32 devices in a mesh: seq: 8 (over y, x, core), wa: 4 (over z).
Axes of the slice: x: 2, y: 2, z: 4, core: 2. Of those that a mesh axis runs over, the one named last changes fastest.
Arguments:
- tokens: bfloat16 [8, 2048, 1792], P(None, ('seq', 'wa')), may hold values from -6 to 6
- cotangent: bfloat16 [8, 2048, 1792], P(None, ('seq', 'wa')), may hold values from -6 to 6
- lengths: int32 [8], replicated, may hold values from 1 to 2048, 10240 in all
- adapter_ids: int32 [8], replicated, may hold values from 0 to 7
- gain_first: float32 [1792], replicated, may hold values from 0.5 to 1.5
- gain_second: float32 [1792], replicated, may hold values from 0.5 to 1.5
- conv_kernel: bfloat16 [3, 1792], replicated, may hold values from -0.625 to 0.625
- mixer_in: bfloat16 [1792, 4096], P(None, 'wa'), may hold values from -0.125 to 0.125
- mixer_out: bfloat16 [1792, 1792], P('wa'), may hold values from -3 to 3
- gate_up: bfloat16 [2, 1792, 4864], P(None, None, 'wa'), may hold values from -0.125 to 0.125
- down_weight: bfloat16 [4864, 1792], P('wa'), may hold values from -0.078125 to 0.078125
- inward_down: bfloat16 [8, 16, 1792], replicated, may hold values from -0.125 to 0.125
- inward_up: bfloat16 [8, 16, 4096], P(None, None, 'wa'), may hold values from -1.5 to 1.5
- outward_down: bfloat16 [8, 16, 1792], P(None, None, 'wa'), may hold values from -3 to 3
- outward_up: bfloat16 [8, 16, 1792], replicated, may hold values from -1.5 to 1.5
- expand_down: bfloat16 [8, 16, 1792], replicated, may hold values from -0.125 to 0.125
- expand_up: bfloat16 [8, 16, 2, 4864], P(None, None, None, 'wa'), may hold values from -1.5 to 1.5
- reduce_down: bfloat16 [8, 16, 4864], P(None, None, 'wa'), may hold values from -0.078125 to 0.078125
- reduce_up: bfloat16 [8, 16, 1792], replicated, may hold values from -1.5 to 1.5
Outputs:
- output: float32 [8, 2048, 1792], P(None, ('seq', 'wa'))
- input_grad: float32 [8, 2048, 1792], P(None, ('seq', 'wa'))
- grad_inward_down: float32 [8, 16, 1792], P(None, None, 'wa')
- grad_inward_up: float32 [8, 16, 4096], P(None, None, 'wa')
- grad_outward_down: float32 [8, 16, 1792], P(None, None, 'wa')
- grad_outward_up: float32 [8, 16, 1792], P(None, None, 'wa')
- grad_expand_down: float32 [8, 16, 1792], P(None, None, 'wa')
- grad_expand_up: float32 [8, 16, 2, 4864], P(None, None, None, 'wa')
- grad_reduce_down: float32 [8, 16, 4864], P(None, None, 'wa')
- grad_reduce_up: float32 [8, 16, 1792], P(None, None, 'wa')
The draws below stay inside these ranges and needn't reach their ends.
Inputs may be any that keep to these rules, and one draw needn't show every extreme that they name: Sequence s holds lengths[s] valid tokens from its start; together the lengths fill 5 * 2048 slots, and one sequence fills all 2048.
All inputs are finite; a program needn't handle non-finite values.
Results may differ from the reference program's by a relative error of at most 0.023.
Values may be sent and summed in bfloat16 or wider, within the bound.
No kernel may reach another device: no remote copies, remote signals or barrier semaphores. Data moves between devices by JAX's collectives and lax.ppermute only.
A program may use at most 256 MiB of HBM per device.

```python
import math
import jax
import jax.numpy as jnp
import numpy as np
from jax import lax

D = 1792
HEADS = 16
HEAD = 112
FEAT = 16
FF = 4864
RANK = 16
ADAPT = 8
SEQS = 8
PACK = 256
SLOTS = 2048


def set_ends(drawn, rng, least, top_value):
    dims = drawn.shape
    spot = [jax.random.randint(jax.random.fold_in(rng, axis), (), 0, dims[axis]) for axis in range(len(dims))]
    drawn = drawn.at[tuple(spot)].set(least)
    longest = dims.index(max(dims))
    spot[longest] = (spot[longest] + 1) % dims[longest]
    return drawn.at[tuple(spot)].set(top_value)


def block_scale(own_key, extent, cuts, low, largest):
    gain, own = 1.0, jax.random.fold_in(own_key, 6)
    for axis_at, shards_of in cuts:
        heights = jnp.exp(jax.random.uniform(jax.random.fold_in(own, axis_at), (shards_of,), jnp.float32, low / len(cuts), largest / len(cuts)))
        gain = gain * jnp.repeat(heights, extent[axis_at] // shards_of).reshape([-1 if axis == axis_at else 1 for axis in range(len(extent))])
    return gain


def split_up(count, total, reach, skew):
    portions = [(1 << 20) // math.isqrt(grade ** skew) + 1 for grade in range(2, count + 1)]
    surplus, holding = total - reach - (count - 1), [1] * (count - 1)
    while surplus > 0:
        candidates = [i for i in range(count - 1) if holding[i] < reach]
        pool, budget = sum([portions[i] for i in candidates]), surplus
        for i in candidates:
            addition = min(reach - holding[i], max(1, budget * portions[i] // pool), surplus)
            holding[i] = holding[i] + addition
            surplus = surplus - addition
    return np.array([reach] + holding)


def uneven_parts(key, number_of, total, bound, slope):
    if number_of == 2:
        one = jax.random.randint(key, (), max(1, total - bound), min(bound, total - 1) + 1)
        return jnp.stack([one, total - one])
    tallies = jnp.asarray(split_up(number_of, total, bound, slope), jnp.int32)
    couples = (number_of - 1) // 2
    giver, sink = tallies[1:1 + 2 * couples:2], tallies[2:2 + 2 * couples:2]
    margin = jnp.minimum(giver - 1, bound - sink)
    shifted = jax.random.randint(jax.random.fold_in(key, 1), (couples,), 0, 1 << 20) % (margin + 1)
    tallies = tallies.at[1:1 + 2 * couples:2].set(giver - shifted).at[2:2 + 2 * couples:2].set(sink + shifted)
    return tallies[jax.random.permutation(jax.random.fold_in(key, 2), number_of)]


def noise(stream_key, extent, deviation, most, shards=(), kind=jnp.bfloat16):
    values = jax.random.normal(stream_key, extent, jnp.float32) * deviation
    if len(shards) > 0:
        values = block_scale(stream_key, extent, shards, -0.22, 0.18) * values
    return jnp.clip(values, min=-most, max=most).astype(kind)


def setup_inputs(seed: int = 0) -> dict:
    keys = jax.random.split(jax.random.key(seed), 20)
    return {
        "tokens": noise(keys[0], (SEQS, SLOTS, D), 1.0, 6.0, ((1, 32),)),
        "cotangent": noise(keys[1], (SEQS, SLOTS, D), 1.0, 6.0, ((1, 32),)),
        "lengths": uneven_parts(keys[2], SEQS, 5 * SLOTS, SLOTS, 1).astype(jnp.int32),
        "adapter_ids": set_ends(jax.random.randint(keys[3], (SEQS,), 0, ADAPT), jax.random.fold_in(keys[3], 1), 0, ADAPT - 1).astype(jnp.int32),
        "gain_first": jnp.clip(1.0 + 0.1 * jax.random.normal(keys[4], (D,), jnp.float32), 0.5, 1.5),
        "gain_second": jnp.clip(1.0 + 0.1 * jax.random.normal(keys[5], (D,), jnp.float32), 0.5, 1.5),
        "conv_kernel": noise(keys[6], (3, D), 0.04, 0.625),
        "mixer_in": noise(keys[7], (D, HEADS * PACK), D ** -0.5, 0.125, ((1, 4),)),
        "mixer_out": noise(keys[8], (D, D), (max(D // 400, 1)) ** -0.5, 3.0, ((0, 4),)),
        "gate_up": noise(keys[9], (2, D, FF), D ** -0.5, 0.125, ((2, 4),)),
        "down_weight": noise(keys[10], (FF, D), FF ** -0.5, 0.078125, ((0, 4),)),
        "inward_down": noise(keys[11], (ADAPT, RANK, D), D ** -0.5, 0.125),
        "inward_up": noise(keys[12], (ADAPT, RANK, HEADS * PACK), RANK ** -0.5, 1.5, ((2, 4),)),
        "outward_down": noise(keys[13], (ADAPT, RANK, D), (max(D // 400, 1)) ** -0.5, 3.0, ((2, 4),)),
        "outward_up": noise(keys[14], (ADAPT, RANK, D), RANK ** -0.5, 1.5),
        "expand_down": noise(keys[15], (ADAPT, RANK, D), D ** -0.5, 0.125),
        "expand_up": noise(keys[16], (ADAPT, RANK, 2, FF), RANK ** -0.5, 1.5, ((3, 4),)),
        "reduce_down": noise(keys[17], (ADAPT, RANK, FF), FF ** -0.5, 0.078125, ((2, 4),)),
        "reduce_up": noise(keys[18], (ADAPT, RANK, D), RANK ** -0.5, 1.5),
    }


EPSILON = 1e-05
HIGHEST = lax.Precision.HIGHEST

@jax.custom_vjp
def low(v):
    return lax.optimization_barrier(v.astype(jnp.bfloat16)).astype(jnp.float32)

@jax.custom_vjp
def low_back(v):
    return v

def low_keep(v):
    return (low(v), None)

def low_pass(kept, grad):
    return (grad,)

def back_keep(v):
    return (v, None)

def back_low(kept, grad):
    return (low(grad),)
low.defvjp(low_keep, low_pass)
low_back.defvjp(back_keep, back_low)

def matmul(operand_one, operand_two):
    return jnp.dot(operand_one, operand_two, precision=HIGHEST)

def rms_norm(values, scale_gain):
    return values * lax.rsqrt(lax.optimization_barrier(jnp.mean(values * values, axis=-1, keepdims=True)) + EPSILON) * scale_gain

def feature_map(values):
    row_count = values.shape[0]
    products = (values[:, :, None] * values[:, None, :]).reshape(row_count, -1) * (1.0 / math.sqrt(2.0))
    return jnp.concatenate([jnp.ones((row_count, 1), jnp.float32), values, products], axis=1)

def taylor_head(query_part, key_part, value_part, keep_mask):
    length = query_part.shape[0]
    block_rows = math.gcd(512, length)
    block_count = length // block_rows
    causal = jnp.tril(jnp.ones((block_rows, block_rows), jnp.float32))
    feature_width = 1 + query_part.shape[1] + query_part.shape[1] * query_part.shape[1]

    def advance(running, pieces):
        memory, normalizer = running
        query_block, key_block, value_block, keep_block = pieces
        scores = jnp.dot(query_block, key_block.T, precision=HIGHEST)
        weight = (1.0 + scores + 0.5 * scores * scores) * causal * keep_block[None, :]
        query_feat = feature_map(query_block)
        key_feat = feature_map(key_block) * keep_block[:, None]
        numerator = jnp.dot(weight, value_block, precision=HIGHEST) + jnp.dot(query_feat, memory, precision=HIGHEST)
        denominator = lax.optimization_barrier(jnp.sum(weight, axis=1)) + jnp.dot(query_feat, normalizer, precision=HIGHEST)
        memory = memory + jnp.dot(key_feat.T, value_block, precision=HIGHEST)
        normalizer = normalizer + lax.optimization_barrier(jnp.sum(key_feat, axis=0))
        return ((memory, normalizer), numerator / denominator[:, None])
    pieces = (0.5 * query_part.reshape(block_count, block_rows, -1), 0.5 * key_part.reshape(block_count, block_rows, -1), value_part.reshape(block_count, block_rows, -1), keep_mask.reshape(block_count, block_rows))
    start = (jnp.zeros((feature_width, value_part.shape[1]), jnp.float32), jnp.zeros((feature_width,), jnp.float32))
    _, result = lax.scan(jax.checkpoint(advance), start, pieces)
    return result.reshape(length, -1)

def mixer_head(packed, kernel, keep_mask):
    query_part = packed[:, :FEAT]
    key_part = packed[:, FEAT:2 * FEAT]
    value_part = packed[:, 2 * FEAT:2 * FEAT + HEAD]
    gate_part = packed[:, 2 * FEAT + HEAD:]
    attended = taylor_head(query_part, key_part, value_part, keep_mask)
    shifted_one = jnp.pad(value_part, ((1, 0), (0, 0)))[:-1]
    shifted_two = jnp.pad(value_part, ((2, 0), (0, 0)))[:-2]
    convolved = kernel[0] * value_part + kernel[1] * shifted_one + kernel[2] * shifted_two
    return attended + convolved * jax.nn.silu(gate_part)

def block_forward(inputs, adapter_hot, keep_mask, gain_first, gain_second, conv_kernel, mixer_in, mixer_out, gate_up, down_weight, inward_down, inward_up, outward_down, outward_up, expand_down, expand_up, reduce_down, reduce_up):

    def select(table):
        return jnp.tensordot(adapter_hot, table, axes=1, precision=HIGHEST)
    length = inputs.shape[0]
    normed = low(rms_norm(inputs, gain_first))
    enter_rank = low(matmul(normed, select(inward_down).T))
    packed = low_back(low(matmul(normed, mixer_in) + matmul(enter_rank, select(inward_up))))
    per_head = packed.reshape(length, HEADS, PACK).transpose(1, 0, 2)
    kernels = conv_kernel.reshape(3, HEADS, HEAD).transpose(1, 0, 2)
    mixed = jax.vmap(mixer_head, in_axes=(0, 0, None))(per_head, kernels, keep_mask)
    mixed = low_back(low(mixed.transpose(1, 0, 2).reshape(length, D)))
    leave_rank = low_back(low(matmul(mixed, select(outward_down).T)))
    branch = low_back(matmul(mixed, mixer_out) + matmul(leave_rank, select(outward_up)))
    residual = inputs + branch
    normed_two = low(rms_norm(residual, gain_second))
    expand_rank = low(matmul(normed_two, select(expand_down).T))
    chosen = select(expand_up)
    gating = low_back(matmul(normed_two, gate_up[0]) + matmul(expand_rank, chosen[:, 0]))
    upward = low_back(matmul(normed_two, gate_up[1]) + matmul(expand_rank, chosen[:, 1]))
    hidden = low(jax.nn.silu(gating) * upward)
    reduce_rank = low_back(low(matmul(hidden, select(reduce_down).T)))
    feed_out = low_back(matmul(hidden, down_weight) + matmul(reduce_rank, select(reduce_up)))
    return keep_mask[:, None] * (residual + feed_out)

def reference(tokens, cotangent, lengths, adapter_ids, gain_first, gain_second, conv_kernel, mixer_in, mixer_out, gate_up, down_weight, inward_down, inward_up, outward_down, outward_up, expand_down, expand_up, reduce_down, reduce_up):
    frozen = tuple((table.astype(jnp.float32) for table in (gain_first, gain_second, conv_kernel, mixer_in, mixer_out, gate_up, down_weight)))
    adapters = tuple((table.astype(jnp.float32) for table in (inward_down, inward_up, outward_down, outward_up, expand_down, expand_up, reduce_down, reduce_up)))
    positions = jnp.arange(tokens.shape[1], dtype=jnp.int32)
    adapter_range = jnp.arange(ADAPT, dtype=jnp.int32)

    def per_sequence(running, sequence_data):
        row_tokens, row_cotangent, length, adapter_id = sequence_data
        keep_mask = (positions < length).astype(jnp.float32)
        adapter_hot = (adapter_range == adapter_id).astype(jnp.float32)

        def forward(inputs, adapt):
            return block_forward(inputs, adapter_hot, keep_mask, frozen[0], frozen[1], frozen[2], frozen[3], frozen[4], frozen[5], frozen[6], adapt[0], adapt[1], adapt[2], adapt[3], adapt[4], adapt[5], adapt[6], adapt[7])
        result, pull = jax.vjp(forward, row_tokens.astype(jnp.float32), adapters)
        input_grad, adapter_grad = pull(row_cotangent.astype(jnp.float32))
        running = jax.tree.map(lambda total_grad, piece_grad: total_grad + piece_grad, running, adapter_grad)
        return (running, (result, input_grad))
    zeros = tuple((jnp.zeros(table.shape, jnp.float32) for table in adapters))
    totals, (outputs, input_grads) = lax.scan(per_sequence, zeros, (tokens, cotangent, lengths, adapter_ids))
    return (outputs, input_grads, totals[0], totals[1], totals[2], totals[3], totals[4], totals[5], totals[6], totals[7])
```

```python
import math

import jax
import jax.numpy as jnp
import numpy as np
from jax import lax
from jax.experimental import pallas as pl
from jax.experimental.pallas import tpu as pltpu
from jax.sharding import Mesh
from jax.sharding import PartitionSpec as P

HEADS = 16
HEAD = 112
FEAT = 16
PACK = 256
PAD = 128
PAIRS = 160
ONE_LANE = HEAD

EPSILON = 1e-05
BF = jnp.bfloat16
F32 = jnp.float32

CHIPS = ("g", "b", "a")
PLANE = ("b", "a", "c")
COLUMN = ("c", "wa")
EVERY = ("g", "b", "a", "c", "wa")


def constants():
    pairs = [(i, j) for i in range(FEAT + 1) for j in range(i, FEAT + 1)]
    table = {}
    for name, lane in (("q", 0), ("k", FEAT)):
        first = np.zeros((PACK, PAIRS), np.float32)
        second = np.zeros((PACK, PAIRS), np.float32)
        for f, (i, j) in enumerate(pairs):
            if i > 0:
                first[lane + i - 1, f] = 0.5
            if j > 0:
                second[lane + j - 1, f] = 0.5
        table["first_" + name] = first
        table["second_" + name] = second
    ones = np.zeros((3, PAIRS), np.float32)
    for f, (i, j) in enumerate(pairs):
        ones[0, f] = 1.0 if i == 0 else 0.0
        ones[1, f] = 1.0 if j == 0 else 0.0
        ones[2, f] = 0.5 if i == j and i > 0 else 1.0
    value = np.zeros((PACK, PAD), np.float32)
    gate = np.zeros((PACK, PAD), np.float32)
    for i in range(HEAD):
        value[2 * FEAT + i, i] = 1.0
        gate[2 * FEAT + HEAD + i, i] = 1.0
    key = np.zeros((PACK, PAD), np.float32)
    query = np.zeros((PACK, PAD), np.float32)
    for i in range(FEAT):
        key[FEAT + i, i] = 0.25
        query[i, FEAT + i] = 0.25
    table.update(value=value, gate=gate, key=key, query=query)
    return {k: jnp.asarray(v, BF) for k, v in table.items()}, jnp.asarray(ones)


def nn(left, right):
    return lax.dot_general(left, right, (((1,), (0,)), ((), ())), preferred_element_type=F32)


def nt(left, right):
    return lax.dot_general(left, right, (((1,), (1,)), ((), ())), preferred_element_type=F32)


def lanes(shape):
    return lax.broadcasted_iota(jnp.int32, shape, 1)


def rows_of(shape):
    return lax.broadcasted_iota(jnp.int32, shape, 0)


def augmented(block, value_ref):
    value = nn(block, value_ref[...])
    return jnp.where(lanes(value.shape) == ONE_LANE, 1.0, value)


def shift_down(values, halo, by):
    rolled = pltpu.roll(values, by, 0)
    place = rows_of(values.shape)
    for row in range(by):
        rolled = jnp.where(place == row, halo[8 - by + row : 9 - by + row, :], rolled)
    return rolled


def shift_up(values, halo, by):
    count = values.shape[0]
    rolled = pltpu.roll(values, count - by, 0)
    place = rows_of(values.shape)
    for row in range(by):
        rolled = jnp.where(place == count - by + row, halo[row : row + 1, :], rolled)
    return rolled


def sigmoid(values):
    return 1.0 / (1.0 + jnp.exp(-values))


def state_kernel(block_ref, keep_ref, first_ref, second_ref, ones_ref, value_ref, out_ref):
    block = block_ref[...]
    first = nt(first_ref[...], block) + ones_ref[:, 0:1]
    second = nt(second_ref[...], block) + ones_ref[:, 1:2]
    features = (first * second * keep_ref[...]).astype(BF)
    out_ref[0] = nn(features, augmented(block, value_ref).astype(BF))


def mixer_kernel(
    block_ref, keep_ref, state_ref, halo_ref, taps_ref, first_ref, second_ref, ones_ref,
    value_ref, gate_ref, key_ref, mixed_ref, kept_ref,
):
    block = block_ref[...]
    rows = block.shape[0]
    half = rows // 2
    first = nn(block, first_ref[...]) + ones_ref[0:1, :]
    second = nn(block, second_ref[...]) + ones_ref[1:2, :]
    features = (first * second * ones_ref[2:3, :]).astype(BF)
    value = augmented(block, value_ref)
    value_low = value.astype(BF)
    key = nn(block, key_ref[...]).astype(BF)
    low_lanes = block[:, :PAD]
    query = jnp.where(lanes(low_lanes.shape) < FEAT, low_lanes, jnp.zeros_like(low_lanes))
    past = nn(features, state_ref[0])
    causal = rows_of((half, half)) >= lanes((half, half))
    sums = []
    for r in range(2):
        total = past[r * half : (r + 1) * half]
        for c in range(r + 1):
            score = 1.0 + nt(query[r * half : (r + 1) * half], key[c * half : (c + 1) * half])
            weight = (0.5 * score * score + 0.5) * keep_ref[:, c * half : (c + 1) * half]
            if r == c:
                weight = jnp.where(causal, weight, 0.0)
            total = total + nn(weight.astype(BF), value_low[c * half : (c + 1) * half])
        sums.append(total)
    total = jnp.concatenate(sums, axis=0)
    inverse = 1.0 / total[:, ONE_LANE : ONE_LANE + 1]
    attended = total * inverse
    halo = nn(halo_ref[...], value_ref[...])
    convolved = (
        taps_ref[0:1, :] * value
        + taps_ref[1:2, :] * shift_down(value, halo, 1)
        + taps_ref[2:3, :] * shift_down(value, halo, 2)
    )
    gate = nn(block, gate_ref[...])
    mixed = attended + convolved * gate * sigmoid(gate)
    place = lanes(mixed.shape)
    mixed_ref[...] = jnp.where(place < HEAD, mixed, 0.0).astype(BF)
    kept_ref[...] = jnp.where(
        place < HEAD, attended, jnp.where(place == ONE_LANE, inverse, 0.0)
    ).astype(BF)


def back_state_kernel(
    block_ref, kept_ref, grad_ref, first_ref, second_ref, ones_ref, gate_ref, scaled_ref, state_ref, edge_ref,
):
    block = block_ref[...]
    grad = grad_ref[...].astype(F32)
    kept = kept_ref[...].astype(F32)
    place = lanes(grad.shape)
    inverse = kept[:, ONE_LANE : ONE_LANE + 1]
    along = jnp.sum(grad * kept, axis=1, keepdims=True)
    scaled = (jnp.where(place == ONE_LANE, -along, grad) * inverse).astype(BF)
    scaled_ref[...] = scaled
    first = nt(first_ref[...], block) + ones_ref[:, 0:1]
    second = nt(second_ref[...], block) + ones_ref[:, 1:2]
    features = (first * second * ones_ref[:, 2:3]).astype(BF)
    state_ref[0] = nn(features, scaled)
    gate = nn(block[:8], gate_ref[...])
    edge_ref[...] = grad[:8] * gate * sigmoid(gate)


def back_mixer_kernel(
    block_ref, scaled_ref, grad_ref, keep_ref, keep_column_ref, state_ref, later_ref, halo_ref, edge_ref, taps_ref,
    first_q_ref, second_q_ref, first_k_ref, second_k_ref,
    back_first_q_ref, back_second_q_ref, back_first_k_ref, back_second_k_ref,
    ones_ref, value_ref, gate_ref, key_ref, query_ref, back_value_ref, back_gate_ref, out_ref,
):
    block = block_ref[...]
    rows = block.shape[0]
    half = rows // 2
    scaled = scaled_ref[...]
    grad = grad_ref[...].astype(F32)
    keep_column = keep_column_ref[...]
    first_q = (nn(block, first_q_ref[...]) + ones_ref[0:1, :]) * ones_ref[2:3, :]
    second_q = (nn(block, second_q_ref[...]) + ones_ref[1:2, :]) * ones_ref[2:3, :]
    first_k = (nn(block, first_k_ref[...]) + ones_ref[0:1, :]) * keep_column
    second_k = (nn(block, second_k_ref[...]) + ones_ref[1:2, :]) * keep_column
    value = augmented(block, value_ref)
    value_low = value.astype(BF)
    feature_q_grad = nt(scaled, state_ref[0])
    feature_k_grad = nt(value_low, later_ref[0])
    pack_grad = (
        nn((feature_q_grad * second_q).astype(BF), back_first_q_ref[...])
        + nn((feature_q_grad * first_q).astype(BF), back_second_q_ref[...])
        + nn((feature_k_grad * second_k).astype(BF), back_first_k_ref[...])
        + nn((feature_k_grad * first_k).astype(BF), back_second_k_ref[...])
    )
    value_grad = nn((first_k * second_k).astype(BF), later_ref[0])
    key = nn(block, key_ref[...]).astype(BF)
    query_after = nn(block, query_ref[...]).astype(BF)
    low_lanes = block[:, :PAD]
    query = jnp.where(lanes(low_lanes.shape) < FEAT, low_lanes, jnp.zeros_like(low_lanes))
    causal = rows_of((half, half)) >= lanes((half, half))
    causal_turned = rows_of((half, half)) <= lanes((half, half))
    query_sums = []
    key_sums = [0.0, 0.0]
    value_sums = [0.0, 0.0]
    for r in range(2):
        here_r = slice(r * half, (r + 1) * half)
        query_sum = 0.0
        for c in range(r + 1):
            here_c = slice(c * half, (c + 1) * half)
            score = 1.0 + nt(query[here_r], key[here_c])
            weight_grad = nt(scaled[here_r], value_low[here_c])
            score_grad = score * weight_grad * keep_ref[:, here_c]
            if r == c:
                score_grad = jnp.where(causal, score_grad, 0.0)
            query_sum = query_sum + nn(score_grad.astype(BF), key[here_c])
            turned = 1.0 + nt(key[here_c], query[here_r])
            turned_grad = nt(value_low[here_c], scaled[here_r]) * turned * keep_column[here_c]
            weight = (0.5 * turned * turned + 0.5) * keep_column[here_c]
            if r == c:
                turned_grad = jnp.where(causal_turned, turned_grad, 0.0)
                weight = jnp.where(causal_turned, weight, 0.0)
            key_sums[c] = key_sums[c] + nn(turned_grad.astype(BF), query_after[here_r])
            value_sums[c] = value_sums[c] + nn(weight.astype(BF), scaled[here_r])
        query_sums.append(query_sum)
    pack_grad = pack_grad + jnp.concatenate(
        [query_sums[0] + key_sums[0], query_sums[1] + key_sums[1]], axis=0
    )
    value_grad = value_grad + jnp.concatenate(value_sums, axis=0)
    halo = nn(halo_ref[...], value_ref[...])
    convolved = (
        taps_ref[0:1, :] * value
        + taps_ref[1:2, :] * shift_down(value, halo, 1)
        + taps_ref[2:3, :] * shift_down(value, halo, 2)
    )
    gate = nn(block, gate_ref[...])
    sig = sigmoid(gate)
    passed = grad * gate * sig
    gate_grad = grad * convolved * sig * (1.0 + gate * (1.0 - sig))
    edge = edge_ref[...]
    value_grad = (
        value_grad
        + taps_ref[0:1, :] * passed
        + taps_ref[1:2, :] * shift_up(passed, edge, 1)
        + taps_ref[2:3, :] * shift_up(passed, edge, 2)
    )
    rest = nn(value_grad.astype(BF), back_value_ref[...]) + nn(
        gate_grad.astype(BF), back_gate_ref[...]
    )
    out_ref[:, :PAD] = (rest[:, :PAD] + pack_grad).astype(BF)
    out_ref[:, PAD:] = rest[:, PAD:].astype(BF)


def whole(shape):
    return pl.BlockSpec(shape, lambda *_: (0,) * len(shape))


def by_column(rows, width):
    return pl.BlockSpec((rows, width), lambda h: (0, h))


def by_head(shape):
    return pl.BlockSpec((1,) + shape, lambda h: (h, 0, 0))


def ffn_kernel(
    normed_ref, top_ref, rank_ref, top_rank_ref, rank_turned_ref, top_rank_turned_ref,
    gate_ref, up_ref, down_ref, expand_gate_ref, expand_up_ref, reduce_ref,
    feed_in_ref, back_in_ref, small_in_ref,
    feed_ref, back_ref, small_ref, expand_gate_grad_ref, expand_up_grad_ref, reduce_grad_ref,
):
    @pl.when(pl.program_id(0) == 0)
    def _():
        feed_ref[...] = feed_in_ref[...]
        back_ref[...] = back_in_ref[...]
        small_ref[...] = small_in_ref[...]

    normed = normed_ref[...]
    rank = rank_ref[...]
    gating = nn(normed, gate_ref[...]) + nn(rank, expand_gate_ref[...])
    upward = nn(normed, up_ref[...]) + nn(rank, expand_up_ref[...])
    hidden_grad = nn(top_ref[...], down_ref[...]) + nn(top_rank_ref[...], reduce_ref[...])
    sig = sigmoid(gating)
    silu = gating * sig
    hidden = (silu * upward).astype(BF)
    up_grad = (hidden_grad * silu).astype(BF)
    gate_grad = (hidden_grad * upward * (sig + silu * (1.0 - sig))).astype(BF)
    feed_ref[...] += nt(hidden, down_ref[...])
    back_ref[...] += nt(gate_grad, gate_ref[...]) + nt(up_grad, up_ref[...])
    small_ref[0] += nt(hidden, reduce_ref[...])
    small_ref[1] += nt(gate_grad, expand_gate_ref[...]) + nt(up_grad, expand_up_ref[...])
    expand_gate_grad_ref[...] = nn(rank_turned_ref[...], gate_grad)
    expand_up_grad_ref[...] = nn(rank_turned_ref[...], up_grad)
    reduce_grad_ref[...] = nn(top_rank_turned_ref[...], hidden)


def ffn_part(normed, top, rank, top_rank, weights, expand_gate, expand_up, reduce, feed, back, small):
    rows, width = normed.shape
    ranks = rank.shape[1]
    hidden = weights.shape[1] // 3
    step = 256
    steps = hidden // step
    once = pl.Buffered(1)

    def fixed(shape):
        return pl.BlockSpec(shape, lambda *_: (0,) * len(shape), pipeline_mode=once)

    def columns(count, offset):
        return pl.BlockSpec((count, step), lambda n: (0, offset + n))

    return pl.pallas_call(
        ffn_kernel,
        grid=(steps,),
        in_specs=[
            fixed((rows, width)), fixed((rows, width)), fixed((rows, ranks)), fixed((rows, ranks)),
            fixed((ranks, rows)), fixed((ranks, rows)),
            columns(width, 0), columns(width, steps), columns(width, 2 * steps),
            columns(ranks, 0), columns(ranks, 0), columns(ranks, 0),
            fixed((rows, width)), fixed((rows, width)), fixed((2, rows, ranks)),
        ],
        out_specs=[
            fixed((rows, width)), fixed((rows, width)), fixed((2, rows, ranks)),
            columns(ranks, 0), columns(ranks, 0), columns(ranks, 0),
        ],
        out_shape=[
            jax.ShapeDtypeStruct((rows, width), F32),
            jax.ShapeDtypeStruct((rows, width), F32),
            jax.ShapeDtypeStruct((2, rows, ranks), F32),
            jax.ShapeDtypeStruct((ranks, hidden), F32),
            jax.ShapeDtypeStruct((ranks, hidden), F32),
            jax.ShapeDtypeStruct((ranks, hidden), F32),
        ],
        input_output_aliases={12: 0, 13: 1, 14: 2},
        name="ffn_part",
    )(normed, top, rank, top_rank, rank.T, top_rank.T, weights, weights, weights, expand_gate, expand_up, reduce, feed, back, small)


def rms(values, gain):
    inverse = lax.rsqrt(jnp.mean(values * values, axis=-1, keepdims=True) + EPSILON)
    return values * inverse * gain


def rms_back(values, gain, upstream):
    inverse = lax.rsqrt(jnp.mean(values * values, axis=-1, keepdims=True) + EPSILON)
    scaled = upstream * gain
    mean = jnp.mean(values * scaled, axis=-1, keepdims=True)
    return inverse * scaled - values * (inverse * inverse * inverse) * mean


def dot(left, right, dims=((1,), (0,))):
    return lax.dot_general(left, right, (dims, ((), ())), preferred_element_type=F32)


ROWS = ((0,), (0,))
TURNED = ((1,), (1,))


def pad_heads(table):
    lead = table.shape[:-1]
    split = table.reshape(lead + (-1, HEAD))
    padded = jnp.pad(split, [(0, 0)] * len(lead) + [(0, 0), (0, PAD - HEAD)])
    return padded.reshape(lead + (-1,))


def unpad_heads(table):
    lead = table.shape[:-1]
    return table.reshape(lead + (-1, PAD))[..., :HEAD].reshape(lead + (-1,))


def on_device(
    tokens, cotangent, lengths, adapter_ids, gain_first, gain_second, conv_kernel, mixer_in, mixer_out, gate_up,
    down_weight, inward_down, inward_up, outward_down, outward_up, expand_down, expand_up, reduce_down, reduce_up,
):
    sequences, slot_rows, width = tokens.shape
    ways = lax.axis_size("wa")
    chips = lax.axis_size("g") * 4
    chip = lax.axis_index(CHIPS)
    core = lax.axis_index("c")
    place = lax.axis_index("wa")
    plane = lax.axis_index(PLANE)
    sequence = core * ways + place
    rows = slot_rows * sequences
    ranks = inward_down.shape[1]
    heads_here = mixer_in.shape[1] // PACK
    out_here = mixer_out.shape[0]
    hidden_here = down_weight.shape[0]
    hidden_pad = -(-hidden_here // 256) * 256 - hidden_here
    next_place = [((d + 1) % ways, d) for d in range(ways)]
    picks, ones = constants()

    def ring(piece):
        return lax.ppermute(piece, "wa", next_place)

    def spread_weights(shard):
        slice_rows = width // 8
        piece = lax.dynamic_slice_in_dim(shard, plane * slice_rows, slice_rows, 0)
        parts = [shard]
        for _ in range(ways - 1):
            piece = ring(piece)
            parts.append(lax.all_gather(piece, PLANE, axis=0, tiled=True))
        return parts

    x = lax.all_to_all(tokens, COLUMN, 0, 0, tiled=True).reshape(rows, width)
    cot = lax.all_to_all(cotangent, COLUMN, 0, 0, tiled=True).reshape(rows, width)

    out_turned = pad_heads(mixer_out.T)
    mixer_weights = spread_weights(jnp.concatenate([mixer_in, out_turned], axis=1))
    ffn_shard = jnp.concatenate(
        [jnp.pad(t, ((0, 0), (0, hidden_pad))) for t in (gate_up[0], gate_up[1], down_weight.T)], axis=1
    )
    ffn_weights = spread_weights(ffn_shard)

    own_tables = (inward_up, outward_down, expand_up.reshape(ADAPTERS(expand_up), ranks, -1), reduce_down)

    def tables_for(target):
        which = adapter_ids[target]
        return jnp.concatenate(
            [lax.dynamic_index_in_dim(t, which, 0, keepdims=False) for t in own_tables], axis=1
        )

    def place_at(step):
        return (place + step) % ways

    tables = [tables_for(sequence)]
    for j in range(1, ways):
        pairs = [(s, (s - j) % ways) for s in range(ways)]
        tables.append(lax.ppermute(tables_for(core * ways + (place - j) % ways), "wa", pairs))
    cut = [inward_up.shape[2], outward_down.shape[2], hidden_here, hidden_here, hidden_here]
    edges = np.cumsum([0] + cut)
    split_tables = [[t[:, edges[n] : edges[n + 1]] for n in range(5)] for t in tables]

    which = adapter_ids[sequence]

    def pick(table):
        return lax.dynamic_index_in_dim(table, which, 0, keepdims=False)

    inward_first, outward_second = pick(inward_down), pick(outward_up)
    expand_first, reduce_second = pick(expand_down), pick(reduce_up)

    positions = chip * rows + jnp.arange(rows, dtype=jnp.int32)
    keep = (positions < lengths[sequence]).astype(F32)
    keep_row, keep_column = keep[None, :], keep[:, None]

    inputs = x.astype(F32)
    normed = rms(inputs, gain_first).astype(BF)
    enter = dot(normed, inward_first, TURNED).astype(BF)
    in_width = mixer_in.shape[1]
    packed = jnp.concatenate(
        [
            (dot(normed, w[:, :in_width]) + dot(enter, t[0])).astype(BF)
            for w, t in zip(mixer_weights, split_tables)
        ],
        axis=1,
    )
    taps = pad_heads(jnp.roll(conv_kernel.astype(F32), -place * out_here, axis=1))
    taps = jnp.pad(taps, ((0, 5), (0, 0)))

    def chip_shift(piece, by):
        pairs = [(i, i + by) for i in range(chips) if 0 <= i + by < chips]
        return lax.ppermute(piece, CHIPS, pairs)

    halo = chip_shift(packed[-8:], 1)

    def scan_chips(local, want_bit):
        before = jnp.zeros_like(local)
        total = local
        bit = 1
        while bit < chips:
            got = lax.ppermute(total.astype(BF), CHIPS, [(i, i ^ bit) for i in range(chips)]).astype(F32)
            take = ((chip & bit) != 0) == want_bit
            before = before + jnp.where(take, got, 0.0)
            total = total + got
            bit *= 2
        return before.astype(BF)

    pairs_shape = (PAIRS, PAD)
    first_q, second_q, first_k, second_k = (picks[n] for n in ("first_q", "second_q", "first_k", "second_k"))
    ones_column = ones.T
    head_params = pltpu.CompilerParams(dimension_semantics=("arbitrary",))
    state = pl.pallas_call(
        state_kernel,
        grid=(HEADS,),
        in_specs=[
            by_column(rows, PACK), whole((1, rows)), whole((PAIRS, PACK)), whole((PAIRS, PACK)), whole((PAIRS, 3)), whole((PACK, PAD)),
        ],
        out_specs=by_head(pairs_shape),
        out_shape=jax.ShapeDtypeStruct((HEADS,) + pairs_shape, F32),
        compiler_params=head_params,
        name="state",
    )(packed, keep_row, first_k.T, second_k.T, ones_column, picks["value"])
    before = scan_chips(state, True)
    mixed, kept = pl.pallas_call(
        mixer_kernel,
        grid=(HEADS,),
        in_specs=[
            by_column(rows, PACK), whole((1, rows)), by_head(pairs_shape), by_column(8, PACK), by_column(8, PAD),
            whole((PACK, PAIRS)), whole((PACK, PAIRS)), whole((3, PAIRS)),
            whole((PACK, PAD)), whole((PACK, PAD)), whole((PACK, PAD)),
        ],
        out_specs=[by_column(rows, PAD), by_column(rows, PAD)],
        out_shape=[jax.ShapeDtypeStruct((rows, HEADS * PAD), BF)] * 2,
        compiler_params=head_params,
        name="mixer",
    )(packed, keep_row, before, halo, taps, first_q, second_q, ones, picks["value"], picks["gate"], picks["key"])

    outward_first = jnp.concatenate([pad_heads(t[1]) for t in split_tables], axis=1)
    out_weights = jnp.concatenate([w[:, in_width:] for w in mixer_weights], axis=1)
    leave = dot(mixed, outward_first, TURNED).astype(BF)
    residual = inputs + dot(mixed, out_weights, TURNED) + dot(leave, outward_second)
    normed_two = rms(residual, gain_second).astype(BF)
    expand = dot(normed_two, expand_first, TURNED).astype(BF)
    top = jnp.where(keep_column > 0, cot, jnp.zeros_like(cot))
    top_rank = dot(top, reduce_second, TURNED).astype(BF)

    feed = jnp.zeros((rows, width), F32)
    back = jnp.zeros((rows, width), F32)
    small = jnp.zeros((2, rows, ranks), F32)
    expand_grads = []
    for w, t in zip(ffn_weights, split_tables):
        padded = [jnp.pad(t[n], ((0, 0), (0, hidden_pad))) for n in (2, 3, 4)]
        feed, back, small, g_gate, g_up, g_reduce = ffn_part(
            normed_two, top, expand, top_rank, w, padded[0], padded[1], padded[2], feed, back, small
        )
        expand_grads.append(
            jnp.concatenate([g_gate[:, :hidden_here], g_up[:, :hidden_here], g_reduce[:, :hidden_here]], axis=1)
        )
    reduce_rank = small[0].astype(BF)
    output = keep_column * (residual + feed + dot(reduce_rank, reduce_second))
    expand_grad = small[1].astype(BF)
    back = back + dot(expand_grad, expand_first)
    grad_reduce_up = dot(reduce_rank, top, ROWS)
    grad_expand_down = dot(expand_grad, normed_two, ROWS)
    residual_grad = top.astype(F32) + rms_back(residual, gain_second, back)
    branch = residual_grad.astype(BF)
    leave_grad = dot(branch, outward_second, TURNED).astype(BF)
    grad_outward_up = dot(leave, branch, ROWS)
    mixed_grad = (dot(branch, out_weights) + dot(leave_grad, outward_first)).astype(BF)
    grad_outward_down = unpad_heads(dot(leave_grad, mixed, ROWS))

    scaled, back_state, edge = pl.pallas_call(
        back_state_kernel,
        grid=(HEADS,),
        in_specs=[
            by_column(rows, PACK), by_column(rows, PAD), by_column(rows, PAD),
            whole((PAIRS, PACK)), whole((PAIRS, PACK)), whole((PAIRS, 3)), whole((PACK, PAD)),
        ],
        out_specs=[by_column(rows, PAD), by_head(pairs_shape), by_column(8, PAD)],
        out_shape=[
            jax.ShapeDtypeStruct((rows, HEADS * PAD), BF),
            jax.ShapeDtypeStruct((HEADS,) + pairs_shape, F32),
            jax.ShapeDtypeStruct((8, HEADS * PAD), F32),
        ],
        compiler_params=head_params,
        name="back_state",
    )(packed, kept, mixed_grad, first_q.T, second_q.T, ones_column, picks["gate"])
    later = scan_chips(back_state, False)
    edge = chip_shift(edge, -1)
    packed_grad = pl.pallas_call(
        back_mixer_kernel,
        grid=(HEADS,),
        in_specs=[
            by_column(rows, PACK), by_column(rows, PAD), by_column(rows, PAD), whole((1, rows)), whole((rows, 1)),
            by_head(pairs_shape), by_head(pairs_shape), by_column(8, PACK), by_column(8, PAD), by_column(8, PAD),
        ]
        + [whole((PACK, PAIRS))] * 4
        + [whole((PAIRS, PAD))] * 4
        + [whole((3, PAIRS))]
        + [whole((PACK, PAD))] * 4
        + [whole((PAD, PACK))] * 2,
        out_specs=by_column(rows, PACK),
        out_shape=jax.ShapeDtypeStruct((rows, HEADS * PACK), BF),
        compiler_params=head_params,
        name="back_mixer",
    )(
        packed, scaled, mixed_grad, keep_row, keep_column, before, later, halo, edge, taps,
        first_q, second_q, first_k, second_k,
        first_q[:PAD].T, second_q[:PAD].T, first_k[:PAD].T, second_k[:PAD].T,
        ones, picks["value"], picks["gate"], picks["key"], picks["query"], picks["value"].T, picks["gate"].T,
    )

    inward_second = jnp.concatenate([t[0] for t in split_tables], axis=1)
    enter_grad = dot(packed_grad, inward_second, TURNED).astype(BF)
    normed_grad = dot(enter_grad, inward_first)
    for j, w in enumerate(mixer_weights):
        normed_grad = normed_grad + dot(packed_grad[:, j * in_width : (j + 1) * in_width], w[:, :in_width], TURNED)
    grad_inward_up = dot(enter, packed_grad, ROWS)
    grad_inward_down = dot(enter_grad, normed, ROWS)
    input_grad = residual_grad + rms_back(inputs, gain_first, normed_grad)

    def send_back(values):
        pieces = values.astype(BF).reshape(sequences, slot_rows, width)
        return lax.all_to_all(pieces, COLUMN, 0, 0, tiled=True).astype(F32)

    seq_hot = (jnp.arange(inward_down.shape[0], dtype=jnp.int32)[:, None] == adapter_ids[None, :]).astype(F32)

    def exchange(pieces):
        got = [pieces(0)]
        for j in range(1, ways):
            pairs = [(s, (s + j) % ways) for s in range(ways)]
            got.append(lax.ppermute(pieces(j).astype(BF), "wa", pairs).astype(F32))
        summed = lax.psum(jnp.stack(got).astype(BF), CHIPS)
        other = lax.ppermute(summed, "c", [(0, 1), (1, 0)])
        hot = jnp.roll(seq_hot.reshape(-1, 2, ways), -place, axis=2)
        hot = jnp.take(hot, (core + jnp.arange(2)) % 2, axis=1)
        order = jnp.array([(-j) % ways for j in range(ways)])
        hot = jnp.take(hot, order, axis=2).reshape(-1, 2 * ways)
        both = jnp.concatenate([summed, other], axis=0).astype(F32)
        return jnp.tensordot(hot, both, axes=1, precision=lax.Precision.HIGHEST)

    def shard_of(table, j):
        size = width // ways
        return lax.dynamic_slice_in_dim(table, place_at(j) * size, size, 1)

    early = exchange(
        lambda j: jnp.concatenate(
            [
                expand_grads[j],
                grad_outward_down[:, j * out_here : (j + 1) * out_here],
                shard_of(grad_outward_up, j),
                shard_of(grad_expand_down, j),
                shard_of(grad_reduce_up, j),
            ],
            axis=1,
        )
    )
    late = exchange(
        lambda j: jnp.concatenate(
            [grad_inward_up[:, j * in_width : (j + 1) * in_width], shard_of(grad_inward_down, j)], axis=1
        )
    )
    shard = width // ways
    at = np.cumsum([0, 2 * hidden_here, hidden_here, out_here, shard, shard, shard])
    early_parts = [early[:, :, at[n] : at[n + 1]] for n in range(6)]
    return (
        send_back(output),
        send_back(input_grad),
        late[:, :, in_width:],
        late[:, :, :in_width],
        early_parts[2],
        early_parts[3],
        early_parts[4],
        early_parts[0].reshape(early.shape[0], ranks, 2, hidden_here),
        early_parts[1],
        early_parts[5],
    )


def ADAPTERS(table):
    return table.shape[0]


def solution(mesh):
    ways = mesh.shape["wa"]
    split = Mesh(mesh.devices.reshape(-1, 2, 2, 2, ways), EVERY)
    slots = P(None, EVERY, None)
    in_specs = (
        slots, slots, P(), P(), P(), P(), P(),
        P(None, "wa"), P("wa", None), P(None, None, "wa"), P("wa", None),
        P(), P(None, None, "wa"), P(None, None, "wa"), P(), P(), P(None, None, None, "wa"), P(None, None, "wa"), P(),
    )
    third = P(None, None, "wa")
    out_specs = (slots, slots, third, third, third, third, third, P(None, None, None, "wa"), third, third)
    return jax.shard_map(on_device, mesh=split, in_specs=in_specs, out_specs=out_specs, check_vma=False)
```

```python
import math

import jax
import jax.numpy as jnp
import numpy as np
from jax import lax
from jax.experimental import pallas as pl
from jax.experimental.pallas import tpu as pltpu
from jax.sharding import Mesh
from jax.sharding import PartitionSpec as P

HEADS = 16
HEAD = 112
FEAT = 16
PACK = 256
PAD = 128
PAIRS = 160
ONE_LANE = HEAD

EPSILON = 1e-05
BF = jnp.bfloat16
F32 = jnp.float32

CHIPS = ("g", "b", "a")
PLANE = ("b", "a", "c")
COLUMN = ("c", "wa")
EVERY = ("g", "b", "a", "c", "wa")


def constants():
    pairs = [(i, j) for i in range(FEAT + 1) for j in range(i, FEAT + 1)]
    first = np.zeros((PAD, PAIRS), np.float32)
    second = np.zeros((PAD, PAIRS), np.float32)
    ones = np.zeros((3, PAIRS), np.float32)
    for f, (i, j) in enumerate(pairs):
        if i > 0:
            first[HEAD + i - 1, f] = 0.5
        if j > 0:
            second[HEAD + j - 1, f] = 0.5
        ones[0, f] = 1.0 if i == 0 else 0.0
        ones[1, f] = 1.0 if j == 0 else 0.0
        ones[2, f] = 0.5 if i == j and i > 0 else 1.0
    order = np.zeros((PACK, PACK), np.float32)
    for i in range(FEAT):
        order[i, HEAD + i] = 1.0
        order[FEAT + i, PAD + HEAD + i] = 1.0
    for i in range(HEAD):
        order[2 * FEAT + i, i] = 1.0
        order[2 * FEAT + HEAD + i, PAD + i] = 1.0
    return jnp.asarray(first, BF), jnp.asarray(second, BF), jnp.asarray(ones), jnp.asarray(order, BF)


def nn(left, right):
    return lax.dot_general(left, right, (((1,), (0,)), ((), ())), preferred_element_type=F32)


def nt(left, right):
    return lax.dot_general(left, right, (((1,), (1,)), ((), ())), preferred_element_type=F32)


def lanes(shape):
    return lax.broadcasted_iota(jnp.int32, shape, 1)


def rows_of(shape):
    return lax.broadcasted_iota(jnp.int32, shape, 0)


def tn(left, right):
    return lax.dot_general(left, right, (((0,), (0,)), ((), ())), preferred_element_type=F32)


def halves(block):
    left, right = block[:, :PAD], block[:, PAD:]
    place = lanes(left.shape)
    zero = jnp.zeros_like(left)
    value = jnp.where(place < HEAD, left, jnp.where(place == ONE_LANE, jnp.ones_like(left), zero))
    query = jnp.where(place < HEAD, zero, left)
    gate = jnp.where(place < HEAD, right, zero)
    key = jnp.where(place < HEAD, zero, right)
    return value, query, gate, key


def shift_down(values, halo, by):
    rolled = pltpu.roll(values, by, 0)
    place = rows_of(values.shape)
    for row in range(by):
        rolled = jnp.where(place == row, halo[8 - by + row : 9 - by + row, :], rolled)
    return rolled


def shift_up(values, halo, by):
    count = values.shape[0]
    rolled = pltpu.roll(values, count - by, 0)
    place = rows_of(values.shape)
    for row in range(by):
        rolled = jnp.where(place == count - by + row, halo[row : row + 1, :], rolled)
    return rolled


def sigmoid(values):
    return 1.0 / (1.0 + jnp.exp(-values))


def state_kernel(block_ref, keep_ref, first_ref, second_ref, ones_ref, out_ref):
    block = block_ref[...]
    right = block[:, PAD:]
    first = nt(first_ref[...], right) + ones_ref[:, 0:1]
    second = nt(second_ref[...], right) + ones_ref[:, 1:2]
    features = (first * second * keep_ref[...]).astype(BF)
    out_ref[0] = nn(features, halves(block)[0])


def inside_kernel(block_ref, keep_column_ref, out_ref):
    value, query, _, key = halves(block_ref[...])
    half = value.shape[0] // 2
    value = value * keep_column_ref[...].astype(BF)
    key = key * 0.25
    causal = rows_of((half, half)) >= lanes((half, half))
    for r in range(2):
        total = 0.0
        for c in range(r + 1):
            score = 1.0 + nt(query[r * half : (r + 1) * half], key[c * half : (c + 1) * half])
            weight = 0.5 * score * score + 0.5
            if r == c:
                weight = jnp.where(causal, weight, 0.0)
            total = total + nn(weight.astype(BF), value[c * half : (c + 1) * half])
        out_ref[r * half : (r + 1) * half, :] = total


def mixer_kernel(
    block_ref, inside_ref, state_ref, halo_ref, taps_ref, first_ref, second_ref, ones_ref, mixed_ref, kept_ref
):
    block = block_ref[...]
    left = block[:, :PAD]
    first = nn(left, first_ref[...]) + ones_ref[0:1, :]
    second = nn(left, second_ref[...]) + ones_ref[1:2, :]
    features = (first * second * ones_ref[2:3, :]).astype(BF)
    value, _, gate, _ = halves(block)
    value, gate = value.astype(F32), gate.astype(F32)
    total = inside_ref[...] + nn(features, state_ref[0])
    inverse = 1.0 / total[:, ONE_LANE : ONE_LANE + 1]
    attended = total * inverse
    halo = halo_ref[:, :PAD].astype(F32)
    convolved = (
        taps_ref[0:1, :] * value
        + taps_ref[1:2, :] * shift_down(value, halo, 1)
        + taps_ref[2:3, :] * shift_down(value, halo, 2)
    )
    mixed = attended + convolved * gate * sigmoid(gate)
    place = lanes(mixed.shape)
    mixed_ref[...] = jnp.where(place < HEAD, mixed, 0.0).astype(BF)
    kept_ref[...] = jnp.where(
        place < HEAD, attended, jnp.where(place == ONE_LANE, inverse, 0.0)
    ).astype(BF)


def back_state_kernel(
    block_ref, kept_ref, grad_ref, first_ref, second_ref, ones_ref, scaled_ref, state_ref, edge_ref
):
    block = block_ref[...]
    grad = grad_ref[...].astype(F32)
    kept = kept_ref[...].astype(F32)
    place = lanes(grad.shape)
    inverse = kept[:, ONE_LANE : ONE_LANE + 1]
    along = jnp.sum(grad * kept, axis=1, keepdims=True)
    scaled = (jnp.where(place == ONE_LANE, -along, grad) * inverse).astype(BF)
    scaled_ref[...] = scaled
    left = block[:, :PAD]
    first = nt(first_ref[...], left) + ones_ref[:, 0:1]
    second = nt(second_ref[...], left) + ones_ref[:, 1:2]
    features = (first * second * ones_ref[:, 2:3]).astype(BF)
    state_ref[0] = nn(features, scaled)
    gate = block[:8, PAD:].astype(F32)
    edge_ref[...] = grad[:8] * gate * sigmoid(gate)


def back_inside_kernel(
    block_ref, scaled_ref, grad_ref, keep_column_ref, state_ref, halo_ref, taps_ref,
    first_ref, second_ref, back_first_ref, back_second_ref, ones_ref, out_ref,
):
    block = block_ref[...]
    rows = block.shape[0]
    half = rows // 2
    scaled = scaled_ref[...]
    grad = grad_ref[...].astype(F32)
    keep_column = keep_column_ref[...]
    value, query, gate, key = halves(block)
    full_value, gate = value.astype(F32), gate.astype(F32)
    value = value * keep_column.astype(BF)
    left = block[:, :PAD]
    first = (nn(left, first_ref[...]) + ones_ref[0:1, :]) * ones_ref[2:3, :]
    second = (nn(left, second_ref[...]) + ones_ref[1:2, :]) * ones_ref[2:3, :]
    feature_grad = nt(scaled, state_ref[0])
    query_grad = nn((feature_grad * second).astype(BF), back_first_ref[...]) + nn(
        (feature_grad * first).astype(BF), back_second_ref[...]
    )
    key = key * 0.25
    query_after = query * 0.25
    causal = rows_of((half, half)) >= lanes((half, half))
    query_sums = []
    key_sums = [0.0, 0.0]
    value_sums = [0.0, 0.0]
    for r in range(2):
        here_r = slice(r * half, (r + 1) * half)
        query_sum = query_grad[here_r]
        for c in range(r + 1):
            here_c = slice(c * half, (c + 1) * half)
            score = 1.0 + nt(query[here_r], key[here_c])
            score_grad = score * nt(scaled[here_r], value[here_c])
            weight = 0.5 * score * score + 0.5
            if r == c:
                score_grad = jnp.where(causal, score_grad, 0.0)
                weight = jnp.where(causal, weight, 0.0)
            score_grad = score_grad.astype(BF)
            query_sum = query_sum + nn(score_grad, key[here_c])
            key_sums[c] = key_sums[c] + tn(score_grad, query_after[here_r])
            value_sums[c] = value_sums[c] + tn(weight.astype(BF), scaled[here_r])
        query_sums.append(query_sum)
    query_grad = jnp.concatenate(query_sums, axis=0)
    key_grad = jnp.concatenate(key_sums, axis=0)
    value_grad = jnp.concatenate(value_sums, axis=0) * keep_column
    halo = halo_ref[:, :PAD].astype(F32)
    convolved = (
        taps_ref[0:1, :] * full_value
        + taps_ref[1:2, :] * shift_down(full_value, halo, 1)
        + taps_ref[2:3, :] * shift_down(full_value, halo, 2)
    )
    sig = sigmoid(gate)
    passed = grad * gate * sig
    gate_grad = grad * convolved * sig * (1.0 + gate * (1.0 - sig))
    nothing = jnp.zeros((8, PAD), F32)
    value_grad = (
        value_grad
        + taps_ref[0:1, :] * passed
        + taps_ref[1:2, :] * shift_up(passed, nothing, 1)
        + taps_ref[2:3, :] * shift_up(passed, nothing, 2)
    )
    place = lanes(query_grad.shape)
    out_ref[:, :PAD] = jnp.where(place < HEAD, value_grad, query_grad).astype(BF)
    out_ref[:, PAD:] = jnp.where(place < HEAD, gate_grad, key_grad).astype(BF)


def back_later_kernel(
    block_ref, part_ref, keep_column_ref, later_ref, edge_ref, taps_ref,
    first_ref, second_ref, back_first_ref, back_second_ref, ones_ref, out_ref,
):
    block = block_ref[...]
    keep_column = keep_column_ref[...]
    right = block[:, PAD:]
    first = (nn(right, first_ref[...]) + ones_ref[0:1, :]) * keep_column
    second = nn(right, second_ref[...]) + ones_ref[1:2, :]
    second_kept = second * keep_column
    later = later_ref[0]
    value = halves(block)[0]
    feature_grad = nt(value, later)
    key_grad = nn((feature_grad * second_kept).astype(BF), back_first_ref[...]) + nn(
        (feature_grad * first).astype(BF), back_second_ref[...]
    )
    value_grad = nn((first * second).astype(BF), later)
    place = lanes(value_grad.shape)
    row = rows_of(value_grad.shape)
    count = block.shape[0]
    edge = edge_ref[...]
    last = taps_ref[1:2, :] * edge[0:1, :] + taps_ref[2:3, :] * edge[1:2, :]
    before_last = taps_ref[2:3, :] * edge[0:1, :]
    value_grad = value_grad + jnp.where(row == count - 1, last, jnp.where(row == count - 2, before_last, 0.0))
    part = part_ref[...].astype(F32)
    out_ref[:, :PAD] = (part[:, :PAD] + jnp.where(place < HEAD, value_grad, 0.0)).astype(BF)
    out_ref[:, PAD:] = (part[:, PAD:] + jnp.where(place < HEAD, 0.0, key_grad)).astype(BF)


def whole(shape):
    return pl.BlockSpec(shape, lambda *_: (0,) * len(shape))


def by_column(rows, width):
    return pl.BlockSpec((rows, width), lambda h: (0, h))


def by_head(shape):
    return pl.BlockSpec((1,) + shape, lambda h: (h, 0, 0))


def ffn_kernel(
    normed_ref, top_ref, rank_ref, top_rank_ref, rank_turned_ref, top_rank_turned_ref,
    gate_ref, up_ref, down_ref, expand_gate_ref, expand_up_ref, reduce_ref,
    feed_in_ref, back_in_ref, small_in_ref,
    feed_ref, back_ref, small_ref, expand_gate_grad_ref, expand_up_grad_ref, reduce_grad_ref,
):
    @pl.when(pl.program_id(0) == 0)
    def _():
        feed_ref[...] = feed_in_ref[...]
        back_ref[...] = back_in_ref[...]
        small_ref[...] = small_in_ref[...]

    normed = normed_ref[...]
    rank = rank_ref[...]
    width = normed.shape[1]
    gate, up, down = (r[...].reshape(-1, width) for r in (gate_ref, up_ref, down_ref))
    expand_gate, expand_up, reduce = expand_gate_ref[0], expand_up_ref[0], reduce_ref[0]
    gating = nt(normed, gate) + nn(rank, expand_gate)
    upward = nt(normed, up) + nn(rank, expand_up)
    hidden_grad = nt(top_ref[...], down) + nn(top_rank_ref[...], reduce)
    sig = sigmoid(gating)
    silu = gating * sig
    hidden = (silu * upward).astype(BF)
    up_grad = (hidden_grad * silu).astype(BF)
    gate_grad = (hidden_grad * upward * (sig + silu * (1.0 - sig))).astype(BF)
    feed_ref[...] += nn(hidden, down)
    back_ref[...] += nn(gate_grad, gate) + nn(up_grad, up)
    small_ref[0] += nt(hidden, reduce)
    small_ref[1] += nt(gate_grad, expand_gate) + nt(up_grad, expand_up)
    expand_gate_grad_ref[0] = nn(rank_turned_ref[...], gate_grad)
    expand_up_grad_ref[0] = nn(rank_turned_ref[...], up_grad)
    reduce_grad_ref[0] = nn(top_rank_turned_ref[...], hidden)


def ffn_part(normed, top, rank, top_rank, weights, weight_specs, tables, feed, back, small):
    rows, width = normed.shape
    ranks = rank.shape[1]
    steps, _, step = tables[0].shape
    once = pl.Buffered(1)

    def fixed(shape):
        return pl.BlockSpec(shape, lambda *_: (0,) * len(shape), pipeline_mode=once)

    by_step = pl.BlockSpec((1, ranks, step), lambda n: (n, 0, 0))
    return pl.pallas_call(
        ffn_kernel,
        grid=(steps,),
        in_specs=[
            fixed((rows, width)), fixed((rows, width)), fixed((rows, ranks)), fixed((rows, ranks)),
            fixed((ranks, rows)), fixed((ranks, rows)),
            *weight_specs,
            by_step, by_step, by_step,
            fixed((rows, width)), fixed((rows, width)), fixed((2, rows, ranks)),
        ],
        out_specs=[
            fixed((rows, width)), fixed((rows, width)), fixed((2, rows, ranks)),
            by_step, by_step, by_step,
        ],
        out_shape=[
            jax.ShapeDtypeStruct((rows, width), F32),
            jax.ShapeDtypeStruct((rows, width), F32),
            jax.ShapeDtypeStruct((2, rows, ranks), F32),
        ]
        + [jax.ShapeDtypeStruct((steps, ranks, step), F32)] * 3,
        input_output_aliases={12: 0, 13: 1, 14: 2},
        name="ffn_part",
    )(normed, top, rank, top_rank, rank.T, top_rank.T, *weights, *tables, feed, back, small)


def rms(values, gain):
    inverse = lax.rsqrt(jnp.mean(values * values, axis=-1, keepdims=True) + EPSILON)
    return values * inverse * gain


def rms_back(values, gain, upstream):
    inverse = lax.rsqrt(jnp.mean(values * values, axis=-1, keepdims=True) + EPSILON)
    scaled = upstream * gain
    mean = jnp.mean(values * scaled, axis=-1, keepdims=True)
    return inverse * scaled - values * (inverse * inverse * inverse) * mean


def dot(left, right, dims=((1,), (0,))):
    return lax.dot_general(left, right, (dims, ((), ())), preferred_element_type=F32)


ROWS = ((0,), (0,))
TURNED = ((1,), (1,))


def pad_heads(table):
    lead = table.shape[:-1]
    split = table.reshape(lead + (-1, HEAD))
    padded = jnp.pad(split, [(0, 0)] * len(lead) + [(0, 0), (0, PAD - HEAD)])
    return padded.reshape(lead + (-1,))


def unpad_heads(table):
    lead = table.shape[:-1]
    return table.reshape(lead + (-1, PAD))[..., :HEAD].reshape(lead + (-1,))


def after(value, *others):
    return lax.optimization_barrier((value,) + others)[0]


SWAP = [(0, 1), (1, 0)]


def on_device(
    tokens, cotangent, lengths, adapter_ids, gain_first, gain_second, conv_kernel, mixer_in, mixer_out, gate_up,
    down_weight, inward_down, inward_up, outward_down, outward_up, expand_down, expand_up, reduce_down, reduce_up,
):
    sequences, slot_rows, width = tokens.shape
    ways = lax.axis_size("wa")
    chips = lax.axis_size("g") * 4
    chip = lax.axis_index(CHIPS)
    core = lax.axis_index("c")
    place = lax.axis_index("wa")
    plane = lax.axis_index(PLANE)
    sequence = core * ways + place
    rows = slot_rows * sequences
    ranks = inward_down.shape[1]
    adapters = inward_down.shape[0]
    in_width = mixer_in.shape[1]
    out_here = mixer_out.shape[0]
    out_width = out_here // HEAD * PAD
    hidden_here = down_weight.shape[0]
    piece_rows = -(-hidden_here // 128) * 16
    hidden_gap = 8 * piece_rows - hidden_here
    gap_at = 7 * piece_rows
    slice_rows = width // 8
    next_place = [((d + 1) % ways, d) for d in range(ways)]
    last_place = [(d, (d + 1) % ways) for d in range(ways)]
    first, second, ones, order = constants()
    barrier = lax.optimization_barrier

    def reorder(columns):
        heads = range(0, columns.shape[1], PACK)
        return jnp.concatenate([dot(columns[:, h : h + PACK], order).astype(BF) for h in heads], axis=1)

    def from_next(piece):
        return lax.ppermute(piece, "wa", next_place)

    def from_last(piece):
        return lax.ppermute(piece, "wa", last_place)

    def opposite(next_piece, last_piece):
        half = next_piece.shape[0] // 2
        return from_next(next_piece[:half]), from_last(last_piece[half:])

    def plane_all(piece):
        return lax.all_gather(piece, PLANE, axis=0, tiled=True)

    def column_exchange(values):
        return lax.all_to_all(values, COLUMN, 0, 0, tiled=True).reshape(rows, width)

    own_in = reorder(lax.dynamic_slice_in_dim(mixer_in, plane * slice_rows, slice_rows, 0))
    own_out = pad_heads(lax.dynamic_slice_in_dim(mixer_out, plane * slice_rows, slice_rows, 1).T)
    mixer_slice = jnp.concatenate([own_in, own_out], axis=1)
    turned_gate_up = jnp.swapaxes(gate_up, 1, 2)
    start = jnp.minimum(plane * piece_rows, hidden_here - piece_rows)
    fresh = plane * piece_rows <= start + jnp.arange(piece_rows)
    gate_up_slice = lax.dynamic_slice(turned_gate_up, (0, start, 0), (2, piece_rows, width))
    down_slice = lax.dynamic_slice_in_dim(down_weight, start, piece_rows, 0)
    ffn_slice = jnp.concatenate([gate_up_slice.reshape(2 * piece_rows, width), down_slice], axis=0)
    ffn_slice = jnp.where(jnp.tile(fresh, 3)[:, None], ffn_slice, 0).astype(BF)

    own_tables = (inward_up, outward_down, expand_up.reshape(adapters, ranks, -1), reduce_down)

    def tables_for(target):
        which = adapter_ids[target]
        return jnp.concatenate(
            [lax.dynamic_index_in_dim(t, which, 0, keepdims=False) for t in own_tables], axis=1
        )

    mixer_1, mixer_3 = barrier((from_next(mixer_slice), from_last(mixer_slice)))
    held = barrier(opposite(mixer_1, mixer_3) + (tokens,))
    mixer_2, tokens_in = jnp.concatenate(held[:2], axis=0), held[2]
    tables = [tables_for(sequence)]
    for j in range(1, ways):
        pairs = [(s, (s - j) % ways) for s in range(ways)]
        tables.append(lax.ppermute(tables_for(core * ways + (place - j) % ways), "wa", pairs))
    mixer_parts = (mixer_1, mixer_2, mixer_3)
    gathered_mixer = plane_all(
        jnp.concatenate([m[:, :in_width] for m in mixer_parts] + [m[:, in_width:] for m in mixer_parts], axis=1)
    )
    cut = [in_width, out_here, hidden_here, hidden_here, hidden_here]
    edges = np.cumsum([0] + cut)
    split_tables = [[t[:, edges[n] : edges[n + 1]] for n in range(5)] for t in tables]
    inward_second = [reorder(t[0]) for t in split_tables]
    outward_first = jnp.concatenate([pad_heads(t[1]) for t in split_tables], axis=1)
    held = barrier(
        (column_exchange(tokens_in), ffn_slice, reorder(mixer_in), pad_heads(mixer_out.T), outward_first)
        + tuple(inward_second)
    )
    x, ffn_slice, in_own, out_own, outward_first = held[:5]
    inward_rest, inward_second = jnp.concatenate(held[6:], axis=1), jnp.concatenate(held[5:], axis=1)
    ffn_1 = from_next(ffn_slice)
    in_split = (ways - 1) * in_width
    in_weights = (in_own, gathered_mixer[:, :in_split])
    out_weights = (out_own, gathered_mixer[:, in_split:])

    which = adapter_ids[sequence]

    def pick(table):
        return lax.dynamic_index_in_dim(table, which, 0, keepdims=False)

    inward_first, outward_second = pick(inward_down), pick(outward_up)
    expand_first, reduce_second = pick(expand_down), pick(reduce_up)
    positions = chip * rows + jnp.arange(rows, dtype=jnp.int32)
    keep = (positions < lengths[sequence]).astype(F32)
    keep_row, keep_column = keep[None, :], keep[:, None]

    inputs = x.astype(F32)
    normed = rms(inputs, gain_first).astype(BF)
    enter = dot(normed, inward_first, TURNED).astype(BF)
    packed_own = (dot(normed, in_own) + dot(enter, held[5])).astype(BF)
    ffn_1, packed_own, ffn_slice = barrier((ffn_1, packed_own, ffn_slice))
    gathered_1 = plane_all(ffn_1)
    ffn_3 = from_last(ffn_slice)
    packed_rest = (dot(normed, in_weights[1]) + dot(enter, inward_rest)).astype(BF)
    packed = jnp.concatenate([packed_own, packed_rest], axis=1)
    taps = pad_heads(jnp.roll(conv_kernel.astype(F32), -place * out_here, axis=1))
    taps = jnp.pad(taps, ((0, 5), (0, 0)))

    def chip_shift(piece, by):
        pairs = [(i, i + by) for i in range(chips) if 0 <= i + by < chips]
        return lax.ppermute(piece, CHIPS, pairs)

    halo = chip_shift(packed[-8:], 1)

    def flip(piece, bit):
        return lax.ppermute(piece, CHIPS, [(i, i ^ bit) for i in range(chips)])

    def scan_chips(local, want_bit):
        before = jnp.zeros_like(local)
        total = local
        bit = 1
        while bit < chips:
            got = flip(total.astype(BF), bit).astype(F32)
            take = ((chip & bit) != 0) == want_bit
            before = before + jnp.where(take, got, 0.0)
            total = total + got
            bit *= 2
        return before.astype(BF)

    pairs_shape = (PAIRS, PAD)
    ones_column = ones.T
    head_params = pltpu.CompilerParams(dimension_semantics=("arbitrary",))
    packed_spec, head_spec = by_column(rows, PACK), by_column(rows, PAD)
    halo_spec, edge_spec, state_spec = by_column(8, PACK), by_column(8, PAD), by_head(pairs_shape)
    turn_specs = [whole((PAIRS, PAD)), whole((PAIRS, PAD)), whole((PAIRS, 3))]
    pick_specs = [whole((PAD, PAIRS)), whole((PAD, PAIRS))]
    back_specs = [whole((PAIRS, PAD)), whole((PAIRS, PAD)), whole((3, PAIRS))]
    narrow = jax.ShapeDtypeStruct((rows, HEADS * PAD), BF)
    packed_shape = jax.ShapeDtypeStruct((rows, HEADS * PACK), BF)
    state_shape = jax.ShapeDtypeStruct((HEADS,) + pairs_shape, F32)

    state = pl.pallas_call(
        state_kernel,
        grid=(HEADS,),
        in_specs=[packed_spec, whole((1, rows))] + turn_specs,
        out_specs=state_spec,
        out_shape=state_shape,
        compiler_params=head_params,
        name="state",
    )(packed, keep_row, first.T, second.T, ones_column)
    ffn_3, cot_in = barrier((ffn_3, cotangent, state))[:2]
    gathered_3 = plane_all(ffn_3)
    cot = column_exchange(cot_in)
    before = scan_chips(state, True)
    inside = pl.pallas_call(
        inside_kernel,
        grid=(HEADS,),
        in_specs=[packed_spec, whole((rows, 1))],
        out_specs=head_spec,
        out_shape=jax.ShapeDtypeStruct((rows, HEADS * PAD), F32),
        compiler_params=head_params,
        name="inside",
    )(packed, keep_column)
    mixed, kept = pl.pallas_call(
        mixer_kernel,
        grid=(HEADS,),
        in_specs=[packed_spec, head_spec, state_spec, halo_spec, edge_spec] + pick_specs + [whole((3, PAIRS))],
        out_specs=[head_spec, head_spec],
        out_shape=[narrow, narrow],
        compiler_params=head_params,
        name="mixer",
    )(packed, inside, before, halo, taps, first, second, ones)

    side_1, side_3, cot = barrier((ffn_1, ffn_3, cot))
    far_parts = opposite(side_1, side_3)
    leave = dot(mixed, outward_first, TURNED).astype(BF)
    residual = inputs + dot(mixed[:, :out_width], out_weights[0], TURNED) + dot(mixed[:, out_width:], out_weights[1], TURNED) + dot(leave, outward_second)
    normed_two = rms(residual, gain_second).astype(BF)
    expand = dot(normed_two, expand_first, TURNED).astype(BF)
    top = jnp.where(keep_column > 0, cot, jnp.zeros_like(cot))
    top_rank = dot(top, reduce_second, TURNED).astype(BF)

    feed = jnp.zeros((rows, width), F32)
    back = jnp.zeros((rows, width), F32)
    small = jnp.zeros((2, rows, ranks), F32)

    def own_spec(which):
        return pl.BlockSpec((1, hidden_here // 2, width), lambda n: (which, n, 0))

    def piece_spec(which):
        return pl.BlockSpec((4, 1, piece_rows, width), lambda n: (n, which, 0, 0))

    specs_for = [piece_spec(t) for t in range(3)]

    def parts_of(gathered):
        return (gathered.reshape(8, 3, piece_rows, width),) * 3

    plans = [
        (0, (turned_gate_up, turned_gate_up, down_weight[None]), [own_spec(0), own_spec(1), own_spec(0)]),
        (1, parts_of(gathered_1), specs_for),
        (3, parts_of(gathered_3), specs_for),
        (2, None, specs_for),
    ]
    expand_grads = [None] * ways
    for j, weights, specs in plans:
        if j == 1:
            held = barrier((feed,) + far_parts)
            feed, gathered_far = held[0], plane_all(jnp.concatenate(held[1:], axis=0))
        if j == 2:
            weights = parts_of(gathered_far)
        chosen = jnp.stack(split_tables[j][2:5])
        if j > 0:
            empty = jnp.zeros((3, ranks, hidden_gap), BF)
            chosen = jnp.concatenate([chosen[..., :gap_at], empty, chosen[..., gap_at:]], axis=2)
        chosen = jnp.swapaxes(chosen.reshape(3, ranks, 2, -1), 1, 2)
        feed, back, small, *grads = ffn_part(
            normed_two, top, expand, top_rank, weights, specs, chosen, feed, back, small
        )
        grads = jnp.swapaxes(jnp.stack(grads), 1, 2).reshape(3, ranks, -1)
        if j > 0:
            grads = jnp.concatenate([grads[..., :gap_at], grads[..., gap_at + hidden_gap :]], axis=2)
        expand_grads[j] = [grads[0], grads[1], grads[2]]
    reduce_rank = small[0].astype(BF)
    output = keep_column * (residual + feed + dot(reduce_rank, reduce_second))
    expand_grad = small[1].astype(BF)
    back = back + dot(expand_grad, expand_first)
    grad_reduce_up = dot(reduce_rank, top, ROWS)
    grad_expand_down = dot(expand_grad, normed_two, ROWS)
    residual_grad = top.astype(F32) + rms_back(residual, gain_second, back)
    branch = residual_grad.astype(BF)
    leave_grad = dot(branch, outward_second, TURNED).astype(BF)
    grad_outward_up = dot(leave, branch, ROWS)
    mixed_grad = jnp.concatenate(
        [
            (dot(branch, w) + dot(leave_grad, t)).astype(BF)
            for w, t in zip(out_weights, (outward_first[:, :out_width], outward_first[:, out_width:]))
        ],
        axis=1,
    )
    grad_outward_down = unpad_heads(dot(leave_grad, mixed, ROWS))

    scaled, back_state, edge = pl.pallas_call(
        back_state_kernel,
        grid=(HEADS,),
        in_specs=[packed_spec, head_spec, head_spec] + turn_specs,
        out_specs=[head_spec, state_spec, edge_spec],
        out_shape=[narrow, state_shape, jax.ShapeDtypeStruct((8, HEADS * PAD), F32)],
        compiler_params=head_params,
        name="back_state",
    )(packed, kept, mixed_grad, first.T, second.T, ones_column)
    later = scan_chips(back_state, False)
    edge = chip_shift(edge, -1)
    part = pl.pallas_call(
        back_inside_kernel,
        grid=(HEADS,),
        in_specs=[packed_spec, head_spec, head_spec, whole((rows, 1)), state_spec, halo_spec, edge_spec]
        + pick_specs
        + back_specs,
        out_specs=packed_spec,
        out_shape=packed_shape,
        compiler_params=head_params,
        name="back_inside",
    )(packed, scaled, mixed_grad, keep_column, before, halo, taps, first, second, first.T, second.T, ones)
    packed_grad = pl.pallas_call(
        back_later_kernel,
        grid=(HEADS,),
        in_specs=[packed_spec, packed_spec, whole((rows, 1)), state_spec, edge_spec, edge_spec]
        + pick_specs
        + back_specs,
        out_specs=packed_spec,
        out_shape=packed_shape,
        compiler_params=head_params,
        name="back_later",
    )(packed, part, keep_column, later, edge, taps, first, second, first.T, second.T, ones)

    enter_grad = dot(packed_grad, inward_second, TURNED).astype(BF)
    normed_grad = (
        dot(packed_grad[:, :in_width], in_weights[0], TURNED)
        + dot(packed_grad[:, in_width:], in_weights[1], TURNED)
        + dot(enter_grad, inward_first)
    )
    input_grad = (branch.astype(F32) + rms_back(inputs, gain_first, normed_grad)).astype(BF)
    input_grad, packed_late = barrier((input_grad, packed_grad))
    grad_inward_up = dot(dot(enter, packed_late, ROWS).astype(BF).reshape(-1, PACK), order, TURNED).astype(BF)
    grad_inward_up = grad_inward_up.reshape(ranks, -1)
    grad_inward_down = dot(after(enter_grad, packed_late), normed, ROWS)

    def send_back(values):
        pieces = values.astype(BF).reshape(sequences, slot_rows, width)
        return lax.all_to_all(pieces, COLUMN, 0, 0, tiled=True).astype(F32)

    hot = (jnp.arange(adapters, dtype=jnp.int32)[:, None] == adapter_ids[None, :]).astype(F32)
    hot = hot.reshape(adapters, 2, ways)
    hot = jnp.where(core == 0, hot, hot[:, ::-1])
    turned = [lax.dynamic_index_in_dim(hot, (place - j) % ways, 2, keepdims=False) for j in range(ways)]
    hot = jnp.stack(turned, axis=2).reshape(adapters, 2 * ways)

    def exchange(pieces):
        got = [pieces(0).astype(BF)]
        for j in range(1, ways):
            pairs = [(s, (s + j) % ways) for s in range(ways)]
            got.append(lax.ppermute(pieces(j).astype(BF), "wa", pairs))
        summed = jnp.stack(got)
        bit = 1
        while bit < chips:
            summed = (summed.astype(F32) + flip(summed, bit).astype(F32)).astype(BF)
            bit *= 2
        both = jnp.concatenate([summed, lax.ppermute(summed, "c", SWAP)], axis=0).astype(F32)
        return jnp.tensordot(hot, both, axes=1, precision=lax.Precision.HIGHEST)

    shard = width // ways

    def shard_of(table, j):
        return lax.dynamic_slice_in_dim(table, (place + j) % ways * shard, shard, 1)

    early = exchange(
        lambda j: after(jnp.concatenate(
            expand_grads[j]
            + [
                grad_outward_down[:, j * out_here : (j + 1) * out_here],
                shard_of(grad_outward_up, j),
                shard_of(grad_expand_down, j),
                shard_of(grad_reduce_up, j),
            ],
            axis=1,
        ), scaled)
    )
    late = exchange(
        lambda j: jnp.concatenate(
            [grad_inward_up[:, j * in_width : (j + 1) * in_width], shard_of(grad_inward_down, j)], axis=1
        )
    )
    at = np.cumsum([0, 2 * hidden_here, hidden_here, out_here, shard, shard, shard])
    early_parts = [early[:, :, at[n] : at[n + 1]] for n in range(6)]
    return (
        send_back(output),
        send_back(input_grad),
        late[:, :, in_width:],
        late[:, :, :in_width],
        early_parts[2],
        early_parts[3],
        early_parts[4],
        early_parts[0].reshape(adapters, ranks, 2, hidden_here),
        early_parts[1],
        early_parts[5],
    )


def solution(mesh):
    ways = mesh.shape["wa"]
    split = Mesh(mesh.devices.reshape(-1, 2, 2, 2, ways), EVERY)
    slots = P(None, EVERY, None)
    in_specs = (
        slots, slots, P(), P(), P(), P(), P(),
        P(None, "wa"), P("wa", None), P(None, None, "wa"), P("wa", None),
        P(), P(None, None, "wa"), P(None, None, "wa"), P(), P(), P(None, None, None, "wa"), P(None, None, "wa"), P(),
    )
    third = P(None, None, "wa")
    out_specs = (slots, slots, third, third, third, third, third, P(None, None, None, "wa"), third, third)
    return jax.shard_map(on_device, mesh=split, in_specs=in_specs, out_specs=out_specs, check_vma=False)
```

```python
import math

import jax
import jax.numpy as jnp
import numpy as np
from jax import lax
from jax.experimental import pallas as pl
from jax.experimental.pallas import tpu as pltpu
from jax.sharding import Mesh
from jax.sharding import PartitionSpec as P

HEADS = 16
HEAD = 112
FEAT = 16
PACK = 256
PAD = 128
PAIRS = 160
ONE_LANE = HEAD

EPSILON = 1e-05
BF = jnp.bfloat16
F32 = jnp.float32

CHIPS = ("g", "b", "a")
PLANE = ("b", "a", "c")
COLUMN = ("c", "wa")
EVERY = ("g", "b", "a", "c", "wa")


def constants():
    pairs = [(i, j) for i in range(FEAT + 1) for j in range(i, FEAT + 1)]
    first = np.zeros((PAD, PAIRS), np.float32)
    second = np.zeros((PAD, PAIRS), np.float32)
    ones = np.zeros((3, PAIRS), np.float32)
    for f, (i, j) in enumerate(pairs):
        if i > 0:
            first[HEAD + i - 1, f] = 0.5
        if j > 0:
            second[HEAD + j - 1, f] = 0.5
        ones[0, f] = 1.0 if i == 0 else 0.0
        ones[1, f] = 1.0 if j == 0 else 0.0
        ones[2, f] = 0.5 if i == j and i > 0 else 1.0
    order = np.zeros((PACK, PACK), np.float32)
    for i in range(FEAT):
        order[i, HEAD + i] = 1.0
        order[FEAT + i, PAD + HEAD + i] = 1.0
    for i in range(HEAD):
        order[2 * FEAT + i, i] = 1.0
        order[2 * FEAT + HEAD + i, PAD + i] = 1.0
    return jnp.asarray(first, BF), jnp.asarray(second, BF), jnp.asarray(ones), jnp.asarray(order, BF)


def nn(left, right):
    return lax.dot_general(left, right, (((1,), (0,)), ((), ())), preferred_element_type=F32)


def nt(left, right):
    return lax.dot_general(left, right, (((1,), (1,)), ((), ())), preferred_element_type=F32)


def lanes(shape):
    return lax.broadcasted_iota(jnp.int32, shape, 1)


def rows_of(shape):
    return lax.broadcasted_iota(jnp.int32, shape, 0)


def tn(left, right):
    return lax.dot_general(left, right, (((0,), (0,)), ((), ())), preferred_element_type=F32)


def halves(block):
    left, right = block[:, :PAD], block[:, PAD:]
    place = lanes(left.shape)
    zero = jnp.zeros_like(left)
    value = jnp.where(place < HEAD, left, jnp.where(place == ONE_LANE, jnp.ones_like(left), zero))
    query = jnp.where(place < HEAD, zero, left)
    gate = jnp.where(place < HEAD, right, zero)
    key = jnp.where(place < HEAD, zero, right)
    return value, query, gate, key


def shift_down(values, halo, by):
    rolled = pltpu.roll(values, by, 0)
    place = rows_of(values.shape)
    for row in range(by):
        rolled = jnp.where(place == row, halo[8 - by + row : 9 - by + row, :], rolled)
    return rolled


def shift_up(values, halo, by):
    count = values.shape[0]
    rolled = pltpu.roll(values, count - by, 0)
    place = rows_of(values.shape)
    for row in range(by):
        rolled = jnp.where(place == count - by + row, halo[row : row + 1, :], rolled)
    return rolled


def sigmoid(values):
    return 1.0 / (1.0 + jnp.exp(-values))


def state_kernel(block_ref, keep_ref, first_ref, second_ref, ones_ref, out_ref):
    block = block_ref[...]
    right = block[:, PAD:]
    first = nt(first_ref[...], right) + ones_ref[:, 0:1]
    second = nt(second_ref[...], right) + ones_ref[:, 1:2]
    features = (first * second * keep_ref[...]).astype(BF)
    out_ref[0] = nn(features, halves(block)[0])


def inside_kernel(block_ref, keep_column_ref, out_ref):
    value, query, _, key = halves(block_ref[...])
    half = value.shape[0] // 2
    value = value * keep_column_ref[...].astype(BF)
    key = key * 0.25
    causal = rows_of((half, half)) >= lanes((half, half))
    for r in range(2):
        total = 0.0
        for c in range(r + 1):
            score = 1.0 + nt(query[r * half : (r + 1) * half], key[c * half : (c + 1) * half])
            weight = 0.5 * score * score + 0.5
            if r == c:
                weight = jnp.where(causal, weight, 0.0)
            total = total + nn(weight.astype(BF), value[c * half : (c + 1) * half])
        out_ref[r * half : (r + 1) * half, :] = total


def mixer_kernel(
    block_ref, inside_ref, state_ref, halo_ref, taps_ref, first_ref, second_ref, ones_ref, mixed_ref, kept_ref
):
    block = block_ref[...]
    left = block[:, :PAD]
    first = nn(left, first_ref[...]) + ones_ref[0:1, :]
    second = nn(left, second_ref[...]) + ones_ref[1:2, :]
    features = (first * second * ones_ref[2:3, :]).astype(BF)
    value, _, gate, _ = halves(block)
    value, gate = value.astype(F32), gate.astype(F32)
    total = inside_ref[...] + nn(features, state_ref[0])
    inverse = 1.0 / total[:, ONE_LANE : ONE_LANE + 1]
    attended = total * inverse
    halo = halo_ref[:, :PAD].astype(F32)
    convolved = (
        taps_ref[0:1, :] * value
        + taps_ref[1:2, :] * shift_down(value, halo, 1)
        + taps_ref[2:3, :] * shift_down(value, halo, 2)
    )
    mixed = attended + convolved * gate * sigmoid(gate)
    place = lanes(mixed.shape)
    mixed_ref[...] = jnp.where(place < HEAD, mixed, 0.0).astype(BF)
    kept_ref[...] = jnp.where(
        place < HEAD, attended, jnp.where(place == ONE_LANE, inverse, 0.0)
    ).astype(BF)


def back_state_kernel(
    block_ref, kept_ref, grad_ref, first_ref, second_ref, ones_ref, scaled_ref, state_ref, edge_ref
):
    block = block_ref[...]
    grad = grad_ref[...].astype(F32)
    kept = kept_ref[...].astype(F32)
    place = lanes(grad.shape)
    inverse = kept[:, ONE_LANE : ONE_LANE + 1]
    along = jnp.sum(grad * kept, axis=1, keepdims=True)
    scaled = (jnp.where(place == ONE_LANE, -along, grad) * inverse).astype(BF)
    scaled_ref[...] = scaled
    left = block[:, :PAD]
    first = nt(first_ref[...], left) + ones_ref[:, 0:1]
    second = nt(second_ref[...], left) + ones_ref[:, 1:2]
    features = (first * second * ones_ref[:, 2:3]).astype(BF)
    state_ref[0] = nn(features, scaled)
    gate = block[:8, PAD:].astype(F32)
    edge_ref[...] = grad[:8] * gate * sigmoid(gate)


def back_inside_kernel(
    block_ref, scaled_ref, grad_ref, keep_column_ref, state_ref, halo_ref, taps_ref,
    first_ref, second_ref, back_first_ref, back_second_ref, ones_ref, out_ref,
):
    block = block_ref[...]
    rows = block.shape[0]
    half = rows // 2
    scaled = scaled_ref[...]
    grad = grad_ref[...].astype(F32)
    keep_column = keep_column_ref[...]
    value, query, gate, key = halves(block)
    full_value, gate = value.astype(F32), gate.astype(F32)
    value = value * keep_column.astype(BF)
    left = block[:, :PAD]
    first = (nn(left, first_ref[...]) + ones_ref[0:1, :]) * ones_ref[2:3, :]
    second = (nn(left, second_ref[...]) + ones_ref[1:2, :]) * ones_ref[2:3, :]
    feature_grad = nt(scaled, state_ref[0])
    query_grad = nn((feature_grad * second).astype(BF), back_first_ref[...]) + nn(
        (feature_grad * first).astype(BF), back_second_ref[...]
    )
    key = key * 0.25
    query_after = query * 0.25
    causal = rows_of((half, half)) >= lanes((half, half))
    query_sums = []
    key_sums = [0.0, 0.0]
    value_sums = [0.0, 0.0]
    for r in range(2):
        here_r = slice(r * half, (r + 1) * half)
        query_sum = query_grad[here_r]
        for c in range(r + 1):
            here_c = slice(c * half, (c + 1) * half)
            score = 1.0 + nt(query[here_r], key[here_c])
            score_grad = score * nt(scaled[here_r], value[here_c])
            weight = 0.5 * score * score + 0.5
            if r == c:
                score_grad = jnp.where(causal, score_grad, 0.0)
                weight = jnp.where(causal, weight, 0.0)
            score_grad = score_grad.astype(BF)
            query_sum = query_sum + nn(score_grad, key[here_c])
            key_sums[c] = key_sums[c] + tn(score_grad, query_after[here_r])
            value_sums[c] = value_sums[c] + tn(weight.astype(BF), scaled[here_r])
        query_sums.append(query_sum)
    query_grad = jnp.concatenate(query_sums, axis=0)
    key_grad = jnp.concatenate(key_sums, axis=0)
    value_grad = jnp.concatenate(value_sums, axis=0) * keep_column
    halo = halo_ref[:, :PAD].astype(F32)
    convolved = (
        taps_ref[0:1, :] * full_value
        + taps_ref[1:2, :] * shift_down(full_value, halo, 1)
        + taps_ref[2:3, :] * shift_down(full_value, halo, 2)
    )
    sig = sigmoid(gate)
    passed = grad * gate * sig
    gate_grad = grad * convolved * sig * (1.0 + gate * (1.0 - sig))
    nothing = jnp.zeros((8, PAD), F32)
    value_grad = (
        value_grad
        + taps_ref[0:1, :] * passed
        + taps_ref[1:2, :] * shift_up(passed, nothing, 1)
        + taps_ref[2:3, :] * shift_up(passed, nothing, 2)
    )
    place = lanes(query_grad.shape)
    out_ref[:, :PAD] = jnp.where(place < HEAD, value_grad, query_grad).astype(BF)
    out_ref[:, PAD:] = jnp.where(place < HEAD, gate_grad, key_grad).astype(BF)


def back_later_kernel(
    block_ref, part_ref, keep_column_ref, later_ref, edge_ref, taps_ref,
    first_ref, second_ref, back_first_ref, back_second_ref, ones_ref, out_ref,
):
    block = block_ref[...]
    keep_column = keep_column_ref[...]
    right = block[:, PAD:]
    first = (nn(right, first_ref[...]) + ones_ref[0:1, :]) * keep_column
    second = nn(right, second_ref[...]) + ones_ref[1:2, :]
    second_kept = second * keep_column
    later = later_ref[0]
    value = halves(block)[0]
    feature_grad = nt(value, later)
    key_grad = nn((feature_grad * second_kept).astype(BF), back_first_ref[...]) + nn(
        (feature_grad * first).astype(BF), back_second_ref[...]
    )
    value_grad = nn((first * second).astype(BF), later)
    place = lanes(value_grad.shape)
    row = rows_of(value_grad.shape)
    count = block.shape[0]
    edge = edge_ref[...]
    last = taps_ref[1:2, :] * edge[0:1, :] + taps_ref[2:3, :] * edge[1:2, :]
    before_last = taps_ref[2:3, :] * edge[0:1, :]
    value_grad = value_grad + jnp.where(row == count - 1, last, jnp.where(row == count - 2, before_last, 0.0))
    part = part_ref[...].astype(F32)
    out_ref[:, :PAD] = (part[:, :PAD] + jnp.where(place < HEAD, value_grad, 0.0)).astype(BF)
    out_ref[:, PAD:] = (part[:, PAD:] + jnp.where(place < HEAD, 0.0, key_grad)).astype(BF)


def whole(shape):
    return pl.BlockSpec(shape, lambda *_: (0,) * len(shape))


def by_column(rows, width):
    return pl.BlockSpec((rows, width), lambda h: (0, h))


def by_head(shape):
    return pl.BlockSpec((1,) + shape, lambda h: (h, 0, 0))


def first_ffn_kernel(*refs):
    @pl.when(pl.program_id(0) == 0)
    def _():
        for ref in refs[12:15]:
            ref[...] = jnp.zeros_like(ref)

    ffn_body(*refs)


def later_ffn_kernel(*refs):
    @pl.when(pl.program_id(0) == 0)
    def _():
        for old, ref in zip(refs[12:15], refs[15:18]):
            ref[...] = old[...]

    ffn_body(*refs[:12], *refs[15:])


def ffn_body(
    normed_ref, top_ref, rank_ref, top_rank_ref, rank_turned_ref, top_rank_turned_ref,
    gate_ref, up_ref, down_ref, expand_gate_ref, expand_up_ref, reduce_ref,
    feed_ref, back_ref, small_ref, expand_gate_grad_ref, expand_up_grad_ref, reduce_grad_ref,
):
    normed = normed_ref[...]
    rank = rank_ref[...]
    width = normed.shape[1]
    gate, up, down = (r[...].reshape(-1, width) for r in (gate_ref, up_ref, down_ref))
    expand_gate, expand_up, reduce = expand_gate_ref[0], expand_up_ref[0], reduce_ref[0]
    gating = nt(normed, gate) + nn(rank, expand_gate)
    upward = nt(normed, up) + nn(rank, expand_up)
    hidden_grad = nt(top_ref[...], down) + nn(top_rank_ref[...], reduce)
    sig = sigmoid(gating)
    silu = gating * sig
    hidden = (silu * upward).astype(BF)
    up_grad = (hidden_grad * silu).astype(BF)
    gate_grad = (hidden_grad * upward * (sig + silu * (1.0 - sig))).astype(BF)
    feed_ref[...] += nn(hidden, down)
    back_ref[...] += nn(gate_grad, gate) + nn(up_grad, up)
    small_ref[0] += nt(hidden, reduce)
    small_ref[1] += nt(gate_grad, expand_gate) + nt(up_grad, expand_up)
    expand_gate_grad_ref[0] = nn(rank_turned_ref[...], gate_grad)
    expand_up_grad_ref[0] = nn(rank_turned_ref[...], up_grad)
    reduce_grad_ref[0] = nn(top_rank_turned_ref[...], hidden)


def ffn_part(normed, top, rank, top_rank, weights, weight_specs, tables, sums):
    rows, width = normed.shape
    ranks = rank.shape[1]
    steps, _, step = tables[0].shape
    once = pl.Buffered(1)

    def fixed(shape):
        return pl.BlockSpec(shape, lambda *_: (0,) * len(shape), pipeline_mode=once)

    by_step = pl.BlockSpec((1, ranks, step), lambda n: (n, 0, 0))
    return pl.pallas_call(
        later_ffn_kernel if sums else first_ffn_kernel,
        grid=(steps,),
        in_specs=[
            fixed((rows, width)), fixed((rows, width)), fixed((rows, ranks)), fixed((rows, ranks)),
            fixed((ranks, rows)), fixed((ranks, rows)),
            *weight_specs,
            by_step, by_step, by_step,
            *([fixed((rows, width)), fixed((rows, width)), fixed((2, rows, ranks))] if sums else []),
        ],
        out_specs=[
            fixed((rows, width)), fixed((rows, width)), fixed((2, rows, ranks)),
            by_step, by_step, by_step,
        ],
        out_shape=[
            jax.ShapeDtypeStruct((rows, width), F32),
            jax.ShapeDtypeStruct((rows, width), F32),
            jax.ShapeDtypeStruct((2, rows, ranks), F32),
        ]
        + [jax.ShapeDtypeStruct((steps, ranks, step), F32)] * 3,
        input_output_aliases={12: 0, 13: 1, 14: 2} if sums else {},
        name="ffn_part",
    )(normed, top, rank, top_rank, rank.T, top_rank.T, *weights, *tables, *sums)


def rms(values, gain):
    inverse = lax.rsqrt(jnp.mean(values * values, axis=-1, keepdims=True) + EPSILON)
    return values * inverse * gain


def rms_back(values, gain, upstream):
    inverse = lax.rsqrt(jnp.mean(values * values, axis=-1, keepdims=True) + EPSILON)
    scaled = upstream * gain
    mean = jnp.mean(values * scaled, axis=-1, keepdims=True)
    return inverse * scaled - values * (inverse * inverse * inverse) * mean


def dot(left, right, dims=((1,), (0,))):
    return lax.dot_general(left, right, (dims, ((), ())), preferred_element_type=F32)


ROWS = ((0,), (0,))
TURNED = ((1,), (1,))


def pad_heads(table):
    lead = table.shape[:-1]
    split = table.reshape(lead + (-1, HEAD))
    padded = jnp.pad(split, [(0, 0)] * len(lead) + [(0, 0), (0, PAD - HEAD)])
    return padded.reshape(lead + (-1,))


def unpad_heads(table):
    lead = table.shape[:-1]
    return table.reshape(lead + (-1, PAD))[..., :HEAD].reshape(lead + (-1,))


def after(value, *others):
    return lax.optimization_barrier((value,) + others)[0]


SWAP = [(0, 1), (1, 0)]


def on_device(
    tokens, cotangent, lengths, adapter_ids, gain_first, gain_second, conv_kernel, mixer_in, mixer_out, gate_up,
    down_weight, inward_down, inward_up, outward_down, outward_up, expand_down, expand_up, reduce_down, reduce_up,
):
    sequences, slot_rows, width = tokens.shape
    ways = lax.axis_size("wa")
    chips = lax.axis_size("g") * 4
    chip = lax.axis_index(CHIPS)
    core = lax.axis_index("c")
    place = lax.axis_index("wa")
    plane = lax.axis_index(PLANE)
    sequence = core * ways + place
    rows = slot_rows * sequences
    ranks = inward_down.shape[1]
    adapters = inward_down.shape[0]
    in_width = mixer_in.shape[1]
    out_here = mixer_out.shape[0]
    out_width = out_here // HEAD * PAD
    hidden_here = down_weight.shape[0]
    piece_rows = -(-hidden_here // 128) * 16
    hidden_gap = 8 * piece_rows - hidden_here
    gap_at = 7 * piece_rows
    slice_rows = width // 8
    next_place = [((d + 1) % ways, d) for d in range(ways)]
    last_place = [(d, (d + 1) % ways) for d in range(ways)]
    first, second, ones, order = constants()
    barrier = lax.optimization_barrier

    def reorder(columns):
        heads = range(0, columns.shape[1], PACK)
        return jnp.concatenate([dot(columns[:, h : h + PACK], order).astype(BF) for h in heads], axis=1)

    def from_next(piece):
        return lax.ppermute(piece, "wa", next_place)

    def from_last(piece):
        return lax.ppermute(piece, "wa", last_place)

    def plane_all(piece):
        return lax.all_gather(piece, PLANE, axis=0, tiled=True)

    def column_exchange(values):
        return lax.all_to_all(values, COLUMN, 0, 0, tiled=True).reshape(rows, width)

    own_in = reorder(lax.dynamic_slice_in_dim(mixer_in, plane * slice_rows, slice_rows, 0))
    own_out = pad_heads(lax.dynamic_slice_in_dim(mixer_out, plane * slice_rows, slice_rows, 1).T)
    mixer_slice = jnp.concatenate([own_in, own_out], axis=1)
    turned_gate_up = jnp.swapaxes(gate_up, 1, 2)
    start = jnp.minimum(plane * piece_rows, hidden_here - piece_rows)
    fresh = plane * piece_rows <= start + jnp.arange(piece_rows)
    gate_up_slice = lax.dynamic_slice(turned_gate_up, (0, start, 0), (2, piece_rows, width))
    down_slice = lax.dynamic_slice_in_dim(down_weight, start, piece_rows, 0)
    ffn_slice = jnp.concatenate([gate_up_slice.reshape(2 * piece_rows, width), down_slice], axis=0)
    ffn_slice = jnp.where(jnp.tile(fresh, 3)[:, None], ffn_slice, 0).astype(BF)

    own_tables = (inward_up, outward_down, expand_up.reshape(adapters, ranks, -1), reduce_down)

    def tables_for(target):
        which = adapter_ids[target]
        return jnp.concatenate(
            [lax.dynamic_index_in_dim(t, which, 0, keepdims=False) for t in own_tables], axis=1
        )

    prepared = [tables_for(sequence)]
    for j in range(1, ways):
        prepared.append(tables_for(core * ways + (place - j) % ways))
    held = barrier((from_next(mixer_slice), mixer_slice, ffn_slice) + tuple(prepared))
    (mixer_1, mixer_slice, ffn_slice), prepared = held[:3], held[3:]
    mixer_2, mixer_3 = from_next(mixer_1), from_last(mixer_slice)
    gathered_near = plane_all(mixer_1)
    tables = [prepared[0]]
    for j in range(1, ways):
        pairs = [(s, (s - j) % ways) for s in range(ways)]
        tables.append(lax.ppermute(prepared[j], "wa", pairs))
    held = barrier((mixer_2, mixer_3, ffn_slice, pad_heads(mixer_out.T)) + tuple(tables[1:]))
    (mixer_2, mixer_3, ffn_slice, out_own), tables[1:] = held[:4], held[4:]
    gathered_rest = plane_all(
        jnp.concatenate(
            [mixer_2[:, :in_width], mixer_3[:, :in_width], mixer_2[:, in_width:], mixer_3[:, in_width:]], axis=1
        )
    )
    cut = [in_width, out_here, hidden_here, hidden_here, hidden_here]
    edges = np.cumsum([0] + cut)
    split_tables = [[t[:, edges[n] : edges[n + 1]] for n in range(5)] for t in tables]
    inward_second = reorder(jnp.concatenate([t[0] for t in split_tables], axis=1))
    outward_first = jnp.concatenate([pad_heads(t[1]) for t in split_tables], axis=1)
    ffn_1, tokens_in, in_own = barrier((from_next(ffn_slice), tokens, reorder(mixer_in)))
    gathered_1 = plane_all(ffn_1)
    in_split = (ways - 2) * in_width
    in_weights = jnp.concatenate([in_own, gathered_near[:, :in_width], gathered_rest[:, :in_split]], axis=1)
    out_weights = jnp.concatenate([out_own, gathered_near[:, in_width:], gathered_rest[:, in_split:]], axis=1)
    x, ffn_slice, in_weights, out_weights, inward_second, outward_first = barrier(
        (column_exchange(tokens_in), ffn_slice, in_weights, out_weights, inward_second, outward_first)
    )
    ffn_3 = from_last(ffn_slice)

    which = adapter_ids[sequence]

    def pick(table):
        return lax.dynamic_index_in_dim(table, which, 0, keepdims=False)

    inward_first, outward_second = pick(inward_down), pick(outward_up)
    expand_first, reduce_second = pick(expand_down), pick(reduce_up)
    positions = chip * rows + jnp.arange(rows, dtype=jnp.int32)
    keep = (positions < lengths[sequence]).astype(F32)
    keep_row, keep_column = keep[None, :], keep[:, None]

    inputs = x.astype(F32)
    normed = rms(inputs, gain_first).astype(BF)
    enter = dot(normed, inward_first, TURNED).astype(BF)
    packed = (dot(normed, in_weights) + dot(enter, inward_second)).astype(BF)
    taps = pad_heads(jnp.roll(conv_kernel.astype(F32), -place * out_here, axis=1))
    taps = jnp.pad(taps, ((0, 5), (0, 0)))

    def chip_shift(piece, by):
        pairs = [(i, i + by) for i in range(chips) if 0 <= i + by < chips]
        return lax.ppermute(piece, CHIPS, pairs)


    def flip(piece, bit, keep_pair=lambda i: True):
        return lax.ppermute(piece, CHIPS, [(i, i ^ bit) for i in range(chips) if keep_pair(i)])

    def scan_chips(local, sent, want_bit, ahead):
        before = jnp.zeros_like(local)
        total = local
        bit = 1
        while bit < chips:
            if bit > 1:
                sent = total.astype(BF)
            if bit == 2:
                sent = ahead(sent)
            last = 2 * bit >= chips
            got = flip(sent, bit, lambda i: not last or ((i & bit) == 0) == want_bit).astype(F32)
            take = ((chip & bit) != 0) == want_bit
            before = before + jnp.where(take, got, 0.0)
            total = total + got
            bit *= 2
        return before.astype(BF)

    pairs_shape = (PAIRS, PAD)
    ones_column = ones.T
    head_params = pltpu.CompilerParams(dimension_semantics=("arbitrary",))
    packed_spec, head_spec = by_column(rows, PACK), by_column(rows, PAD)
    halo_spec, edge_spec, state_spec = by_column(8, PACK), by_column(8, PAD), by_head(pairs_shape)
    turn_specs = [whole((PAIRS, PAD)), whole((PAIRS, PAD)), whole((PAIRS, 3))]
    pick_specs = [whole((PAD, PAIRS)), whole((PAD, PAIRS))]
    back_specs = [whole((PAIRS, PAD)), whole((PAIRS, PAD)), whole((3, PAIRS))]
    narrow = jax.ShapeDtypeStruct((rows, HEADS * PAD), BF)
    packed_shape = jax.ShapeDtypeStruct((rows, HEADS * PACK), BF)
    state_shape = jax.ShapeDtypeStruct((HEADS,) + pairs_shape, F32)

    state = pl.pallas_call(
        state_kernel,
        grid=(HEADS,),
        in_specs=[packed_spec, whole((1, rows))] + turn_specs,
        out_specs=state_spec,
        out_shape=state_shape,
        compiler_params=head_params,
        name="state",
    )(packed, keep_row, first.T, second.T, ones_column)
    state_sent, last_rows = barrier((state.astype(BF), packed[-8:]))
    ffn_3, cot_in, halo = barrier((ffn_3, cotangent, chip_shift(last_rows, 1)))
    gathered_3 = plane_all(ffn_3)
    cot = column_exchange(cot_in)
    before = scan_chips(state, state_sent, True, lambda sent: sent)
    staged = []
    inside = pl.pallas_call(
        inside_kernel,
        grid=(HEADS,),
        in_specs=[packed_spec, whole((rows, 1))],
        out_specs=head_spec,
        out_shape=jax.ShapeDtypeStruct((rows, HEADS * PAD), F32),
        compiler_params=head_params,
        name="inside",
    )(packed, keep_column)
    ffn_1, cot, inside, before = barrier((ffn_1, cot, inside, before))
    ffn_2 = from_next(ffn_1)
    mixed, kept = pl.pallas_call(
        mixer_kernel,
        grid=(HEADS,),
        in_specs=[packed_spec, head_spec, state_spec, halo_spec, edge_spec] + pick_specs + [whole((3, PAIRS))],
        out_specs=[head_spec, head_spec],
        out_shape=[narrow, narrow],
        compiler_params=head_params,
        name="mixer",
    )(packed, inside, before, halo, taps, first, second, ones)

    leave = dot(mixed, outward_first, TURNED).astype(BF)
    residual = inputs + dot(mixed, out_weights, TURNED) + dot(leave, outward_second)
    normed_two = rms(residual, gain_second).astype(BF)
    top = jnp.where(keep_column > 0, cot, jnp.zeros_like(cot))
    top_rank = dot(top, reduce_second, TURNED).astype(BF)
    normed_two, ffn_2, top, top_rank = barrier((normed_two, ffn_2, top, top_rank))
    gathered_far = plane_all(ffn_2)
    expand = dot(normed_two, expand_first, TURNED).astype(BF)

    def own_spec(which):
        return pl.BlockSpec((1, hidden_here // 2, width), lambda n: (which, n, 0))

    def piece_spec(which):
        return pl.BlockSpec((4, 1, piece_rows, width), lambda n: (n, which, 0, 0))

    specs_for = [piece_spec(t) for t in range(3)]

    def parts_of(gathered):
        return (gathered.reshape(8, 3, piece_rows, width),) * 3

    plans = [
        (0, (turned_gate_up, turned_gate_up, down_weight[None]), [own_spec(0), own_spec(1), own_spec(0)]),
        (1, parts_of(gathered_1), specs_for),
        (3, parts_of(gathered_3), specs_for),
        (2, parts_of(gathered_far), specs_for),
    ]
    expand_grads, sums = [None] * ways, ()
    for j, weights, specs in plans:
        chosen = jnp.stack(split_tables[j][2:5])
        if j > 0:
            empty = jnp.zeros((3, ranks, hidden_gap), BF)
            chosen = jnp.concatenate([chosen[..., :gap_at], empty, chosen[..., gap_at:]], axis=2)
        chosen = jnp.swapaxes(chosen.reshape(3, ranks, 2, -1), 1, 2)
        *sums, g_gate, g_up, g_reduce = ffn_part(normed_two, top, expand, top_rank, weights, specs, chosen, tuple(sums))
        sums, grads = tuple(sums), (g_gate, g_up, g_reduce)
        grads = jnp.swapaxes(jnp.stack(grads), 1, 2).reshape(3, ranks, -1)
        if j > 0:
            grads = jnp.concatenate([grads[..., :gap_at], grads[..., gap_at + hidden_gap :]], axis=2)
        expand_grads[j] = [grads[0], grads[1], grads[2]]
    feed, back, small = sums
    reduce_rank = small[0].astype(BF)
    expand_grad = small[1].astype(BF)
    back = back + dot(expand_grad, expand_first)
    grad_reduce_up = dot(reduce_rank, top, ROWS)
    grad_expand_down = dot(expand_grad, normed_two, ROWS)
    residual_grad = top.astype(F32) + rms_back(residual, gain_second, back)
    branch = residual_grad.astype(BF)
    leave_grad = dot(branch, outward_second, TURNED).astype(BF)
    grad_outward_up = dot(leave, branch, ROWS)
    mixed_grad = (dot(branch, out_weights) + dot(leave_grad, outward_first)).astype(BF)
    grad_outward_down = unpad_heads(dot(leave_grad, mixed, ROWS))

    scaled, back_state, edge = pl.pallas_call(
        back_state_kernel,
        grid=(HEADS,),
        in_specs=[packed_spec, head_spec, head_spec] + turn_specs,
        out_specs=[head_spec, state_spec, edge_spec],
        out_shape=[narrow, state_shape, jax.ShapeDtypeStruct((8, HEADS * PAD), F32)],
        compiler_params=head_params,
        name="back_state",
    )(packed, kept, mixed_grad, first.T, second.T, ones_column)
    hot = (jnp.arange(adapters, dtype=jnp.int32)[:, None] == adapter_ids[None, :]).astype(F32)
    hot = hot.reshape(adapters, 2, ways)
    hot = jnp.where(core == 0, hot, hot[:, ::-1])
    turned = [lax.dynamic_index_in_dim(hot, (place - j) % ways, 2, keepdims=False) for j in range(ways)]
    turned = [lax.dynamic_index_in_dim(jnp.stack(turned, axis=2), (chip % 4) ^ k, 2, keepdims=False) for k in range(4)]
    hot = jnp.stack(turned, axis=2).reshape(adapters, 8)
    same_rank = jnp.eye(ranks, dtype=F32)[None, :, None, :]
    hot_rows = (hot[:, None, :, None] * same_rank).reshape(adapters * ranks, 8 * ranks).astype(BF)

    def exchange_places(pieces):
        got = [pieces(0).astype(BF)]
        for j in range(1, ways):
            pairs = [(s, (s + j) % ways) for s in range(ways)]
            got.append(lax.ppermute(pieces(j).astype(BF), "wa", pairs))
        return jnp.stack(got)

    def exchange_chips(table):
        bit = 4
        while bit < chips:
            table = (table.astype(F32) + flip(table, bit).astype(F32)).astype(BF)
            bit *= 2

        def sequence_at(other):
            return lax.dynamic_index_in_dim(table, (chip % 4) ^ other, 0, keepdims=False)

        summed = sum([flip(sequence_at(k), k).astype(F32) for k in range(1, 4)], sequence_at(0).astype(F32)).astype(BF)
        parts = jnp.concatenate([summed] + [flip(summed, k) for k in range(1, 4)], axis=0)
        parts = jnp.concatenate([parts, lax.ppermute(parts, "c", SWAP)], axis=0)
        return dot(hot_rows, parts).reshape(adapters, ranks, -1)

    shard = width // ways

    def shard_of(table, j):
        return lax.dynamic_slice_in_dim(table, (place + j) % ways * shard, shard, 1)

    any_space = pl.BlockSpec(memory_space=pl.ANY)

    def back_inside(base, scaled, old):
        def shift(spec):
            return pl.BlockSpec(spec.block_shape, lambda h, m=spec.index_map: m(h + base))

        return pl.pallas_call(
            back_inside_kernel if old is None else lambda *refs: back_inside_kernel(*refs[:12], refs[-1]),
            grid=(HEADS // 2,),
            in_specs=[
                shift(packed_spec), shift(head_spec), shift(head_spec), whole((rows, 1)),
                shift(state_spec), shift(halo_spec), shift(edge_spec),
            ]
            + pick_specs
            + back_specs
            + ([] if old is None else [any_space]),
            out_specs=shift(packed_spec),
            out_shape=packed_shape,
            input_output_aliases={} if old is None else {12: 0},
            compiler_params=head_params,
            name="back_inside",
        )(
            packed, scaled, mixed_grad, keep_column, before, halo, taps, first, second, first.T, second.T, ones,
            *(() if old is None else (old,)),
        )

    def inside_first(sent):
        sent, part, again, *rest = barrier((sent, back_inside(0, scaled, None), scaled, feed) + outer_grads)
        staged.append((back_inside(HEADS // 2, again, part), rest))
        return sent

    outer_grads = (grad_outward_down, grad_outward_up, grad_expand_down, grad_reduce_up)
    edge = chip_shift(edge, -1)
    later = scan_chips(back_state, back_state.astype(BF), False, inside_first)
    part, (feed, *outer_grads) = staged[0]
    output = (keep_column * (residual + feed + dot(reduce_rank, reduce_second))).astype(BF)

    def send_back(values):
        return lax.all_to_all(values.reshape(sequences, slot_rows, -1), COLUMN, 0, 0, tiled=True)

    packed_grad = pl.pallas_call(
        back_later_kernel,
        grid=(HEADS,),
        in_specs=[packed_spec, packed_spec, whole((rows, 1)), state_spec, edge_spec, edge_spec]
        + pick_specs
        + back_specs,
        out_specs=packed_spec,
        out_shape=packed_shape,
        compiler_params=head_params,
        name="back_later",
    )(packed, part, keep_column, later, edge, taps, first, second, first.T, second.T, ones)

    packed_grad, back_first = barrier((packed_grad, send_back(output[:, : width // 2])))
    back_last = send_back(after(output[:, width // 2 :], back_first))
    enter_grad = dot(packed_grad, inward_second, TURNED).astype(BF)
    normed_grad = (
        dot(packed_grad, in_weights, TURNED) + dot(enter_grad, inward_first)
    )
    input_grad = (branch.astype(F32) + rms_back(inputs, gain_first, normed_grad)).astype(BF)
    grad_inward_up = dot(dot(enter, packed_grad, ROWS).astype(BF).reshape(-1, PACK), order, TURNED).astype(BF)
    grad_inward_up = grad_inward_up.reshape(ranks, -1)
    grad_inward_down = dot(enter_grad, normed, ROWS)

    places = exchange_places(
        lambda j: jnp.concatenate(
            expand_grads[j]
            + [outer_grads[0][:, j * out_here : (j + 1) * out_here]]
            + [shard_of(t, j) for t in outer_grads[1:]]
            + [grad_inward_up[:, j * in_width : (j + 1) * in_width], shard_of(grad_inward_down, j)],
            axis=1,
        )
    )
    input_grad, places, back_last = barrier((input_grad, places, back_last))
    input_first = send_back(input_grad[:, : width // 2])
    input_last = send_back(after(input_grad[:, width // 2 :], input_first))
    sums = exchange_chips(places)
    at = np.cumsum([0, 2 * hidden_here, hidden_here, out_here, shard, shard, shard, in_width, shard])
    grads = [sums[:, :, at[n] : at[n + 1]] for n in range(8)]
    return (
        jnp.concatenate([back_first, back_last], axis=2).astype(F32),
        jnp.concatenate([input_first, input_last], axis=2).astype(F32),
        grads[7],
        grads[6],
        grads[2],
        grads[3],
        grads[4],
        grads[0].reshape(adapters, ranks, 2, hidden_here),
        grads[1],
        grads[5],
    )


def solution(mesh):
    ways = mesh.shape["wa"]
    split = Mesh(mesh.devices.reshape(-1, 2, 2, 2, ways), EVERY)
    slots = P(None, EVERY, None)
    in_specs = (
        slots, slots, P(), P(), P(), P(), P(),
        P(None, "wa"), P("wa", None), P(None, None, "wa"), P("wa", None),
        P(), P(None, None, "wa"), P(None, None, "wa"), P(), P(), P(None, None, None, "wa"), P(None, None, "wa"), P(),
    )
    third = P(None, None, "wa")
    out_specs = (slots, slots, third, third, third, third, third, P(None, None, None, "wa"), third, third)
    return jax.shard_map(on_device, mesh=split, in_specs=in_specs, out_specs=out_specs, check_vma=False)
```

```python
import math

import jax
import jax.numpy as jnp
import numpy as np
from jax import lax
from jax.experimental import pallas as pl
from jax.experimental.pallas import tpu as pltpu
from jax.sharding import Mesh
from jax.sharding import PartitionSpec as P

HEADS = 16
HEAD = 112
FEAT = 16
PACK = 256
PAD = 128
PAIRS = 160
ONE_LANE = HEAD

EPSILON = 1e-05
BF = jnp.bfloat16
F32 = jnp.float32

CHIPS = ("g", "b", "a")
PLANE = ("b", "a", "c")
COLUMN = ("c", "wa")
EVERY = ("g", "b", "a", "c", "wa")


def constants():
    pairs = [(i, j) for i in range(FEAT + 1) for j in range(i, FEAT + 1)]
    first = np.zeros((PAD, PAIRS), np.float32)
    second = np.zeros((PAD, PAIRS), np.float32)
    ones = np.zeros((3, PAIRS), np.float32)
    for f, (i, j) in enumerate(pairs):
        if i > 0:
            first[HEAD + i - 1, f] = 0.5
        if j > 0:
            second[HEAD + j - 1, f] = 0.5
        ones[0, f] = 1.0 if i == 0 else 0.0
        ones[1, f] = 1.0 if j == 0 else 0.0
        ones[2, f] = 0.5 if i == j and i > 0 else 1.0
    order = np.zeros((PACK, PACK), np.float32)
    for i in range(FEAT):
        order[i, HEAD + i] = 1.0
        order[FEAT + i, PAD + HEAD + i] = 1.0
    for i in range(HEAD):
        order[2 * FEAT + i, i] = 1.0
        order[2 * FEAT + HEAD + i, PAD + i] = 1.0
    return jnp.asarray(first, BF), jnp.asarray(second, BF), jnp.asarray(ones), jnp.asarray(order, BF)


def nn(left, right):
    return lax.dot_general(left, right, (((1,), (0,)), ((), ())), preferred_element_type=F32)


def nt(left, right):
    return lax.dot_general(left, right, (((1,), (1,)), ((), ())), preferred_element_type=F32)


def lanes(shape):
    return lax.broadcasted_iota(jnp.int32, shape, 1)


def rows_of(shape):
    return lax.broadcasted_iota(jnp.int32, shape, 0)


def tn(left, right):
    return lax.dot_general(left, right, (((0,), (0,)), ((), ())), preferred_element_type=F32)


def halves(block):
    left, right = block[:, :PAD], block[:, PAD:]
    place = lanes(left.shape)
    zero = jnp.zeros_like(left)
    value = jnp.where(place < HEAD, left, jnp.where(place == ONE_LANE, jnp.ones_like(left), zero))
    query = jnp.where(place < HEAD, zero, left)
    gate = jnp.where(place < HEAD, right, zero)
    key = jnp.where(place < HEAD, zero, right)
    return value, query, gate, key


def shift_down(values, halo, by):
    rolled = pltpu.roll(values, by, 0)
    place = rows_of(values.shape)
    for row in range(by):
        rolled = jnp.where(place == row, halo[8 - by + row : 9 - by + row, :], rolled)
    return rolled


def shift_up(values, halo, by):
    count = values.shape[0]
    rolled = pltpu.roll(values, count - by, 0)
    place = rows_of(values.shape)
    for row in range(by):
        rolled = jnp.where(place == count - by + row, halo[row : row + 1, :], rolled)
    return rolled


def sigmoid(values):
    return 1.0 / (1.0 + jnp.exp(-values))


def state_kernel(block_ref, keep_ref, first_ref, second_ref, ones_ref, out_ref):
    block = block_ref[...]
    right = block[:, PAD:]
    first = nt(first_ref[...], right) + ones_ref[:, 0:1]
    second = nt(second_ref[...], right) + ones_ref[:, 1:2]
    features = (first * second * keep_ref[...]).astype(BF)
    out_ref[0] = nn(features, halves(block)[0])


def inside_kernel(block_ref, keep_column_ref, out_ref):
    value, query, _, key = halves(block_ref[...])
    half = value.shape[0] // 2
    value = value * keep_column_ref[...].astype(BF)
    key = key * 0.25
    causal = rows_of((half, half)) >= lanes((half, half))
    for r in range(2):
        total = 0.0
        for c in range(r + 1):
            score = 1.0 + nt(query[r * half : (r + 1) * half], key[c * half : (c + 1) * half])
            weight = 0.5 * score * score + 0.5
            if r == c:
                weight = jnp.where(causal, weight, 0.0)
            total = total + nn(weight.astype(BF), value[c * half : (c + 1) * half])
        out_ref[r * half : (r + 1) * half, :] = total


def mixer_kernel(
    block_ref, inside_ref, state_ref, halo_ref, taps_ref, first_ref, second_ref, ones_ref, mixed_ref, kept_ref
):
    block = block_ref[...]
    left = block[:, :PAD]
    first = nn(left, first_ref[...]) + ones_ref[0:1, :]
    second = nn(left, second_ref[...]) + ones_ref[1:2, :]
    features = (first * second * ones_ref[2:3, :]).astype(BF)
    value, _, gate, _ = halves(block)
    value, gate = value.astype(F32), gate.astype(F32)
    total = inside_ref[...] + nn(features, state_ref[0])
    inverse = 1.0 / total[:, ONE_LANE : ONE_LANE + 1]
    attended = total * inverse
    halo = halo_ref[:, :PAD].astype(F32)
    convolved = (
        taps_ref[0:1, :] * value
        + taps_ref[1:2, :] * shift_down(value, halo, 1)
        + taps_ref[2:3, :] * shift_down(value, halo, 2)
    )
    mixed = attended + convolved * gate * sigmoid(gate)
    place = lanes(mixed.shape)
    mixed_ref[...] = jnp.where(place < HEAD, mixed, 0.0).astype(BF)
    kept_ref[...] = jnp.where(
        place < HEAD, attended, jnp.where(place == ONE_LANE, inverse, 0.0)
    ).astype(BF)


def back_state_kernel(
    block_ref, kept_ref, grad_ref, first_ref, second_ref, ones_ref, scaled_ref, state_ref, edge_ref
):
    block = block_ref[...]
    grad = grad_ref[...].astype(F32)
    kept = kept_ref[...].astype(F32)
    place = lanes(grad.shape)
    inverse = kept[:, ONE_LANE : ONE_LANE + 1]
    along = jnp.sum(grad * kept, axis=1, keepdims=True)
    scaled = (jnp.where(place == ONE_LANE, -along, grad) * inverse).astype(BF)
    scaled_ref[...] = scaled
    left = block[:, :PAD]
    first = nt(first_ref[...], left) + ones_ref[:, 0:1]
    second = nt(second_ref[...], left) + ones_ref[:, 1:2]
    features = (first * second * ones_ref[:, 2:3]).astype(BF)
    state_ref[0] = nn(features, scaled)
    gate = block[:8, PAD:].astype(F32)
    edge_ref[...] = grad[:8] * gate * sigmoid(gate)


def back_inside_kernel(
    block_ref, scaled_ref, grad_ref, keep_column_ref, state_ref, halo_ref, taps_ref,
    first_ref, second_ref, back_first_ref, back_second_ref, ones_ref, out_ref,
):
    block = block_ref[...]
    rows = block.shape[0]
    half = rows // 2
    scaled = scaled_ref[...]
    grad = grad_ref[...].astype(F32)
    keep_column = keep_column_ref[...]
    value, query, gate, key = halves(block)
    full_value, gate = value.astype(F32), gate.astype(F32)
    value = value * keep_column.astype(BF)
    left = block[:, :PAD]
    first = (nn(left, first_ref[...]) + ones_ref[0:1, :]) * ones_ref[2:3, :]
    second = (nn(left, second_ref[...]) + ones_ref[1:2, :]) * ones_ref[2:3, :]
    feature_grad = nt(scaled, state_ref[0])
    query_grad = nn((feature_grad * second).astype(BF), back_first_ref[...]) + nn(
        (feature_grad * first).astype(BF), back_second_ref[...]
    )
    key = key * 0.25
    query_after = query * 0.25
    causal = rows_of((half, half)) >= lanes((half, half))
    query_sums = []
    key_sums = [0.0, 0.0]
    value_sums = [0.0, 0.0]
    for r in range(2):
        here_r = slice(r * half, (r + 1) * half)
        query_sum = query_grad[here_r]
        for c in range(r + 1):
            here_c = slice(c * half, (c + 1) * half)
            score = 1.0 + nt(query[here_r], key[here_c])
            score_grad = score * nt(scaled[here_r], value[here_c])
            weight = 0.5 * score * score + 0.5
            if r == c:
                score_grad = jnp.where(causal, score_grad, 0.0)
                weight = jnp.where(causal, weight, 0.0)
            score_grad = score_grad.astype(BF)
            query_sum = query_sum + nn(score_grad, key[here_c])
            key_sums[c] = key_sums[c] + tn(score_grad, query_after[here_r])
            value_sums[c] = value_sums[c] + tn(weight.astype(BF), scaled[here_r])
        query_sums.append(query_sum)
    query_grad = jnp.concatenate(query_sums, axis=0)
    key_grad = jnp.concatenate(key_sums, axis=0)
    value_grad = jnp.concatenate(value_sums, axis=0) * keep_column
    halo = halo_ref[:, :PAD].astype(F32)
    convolved = (
        taps_ref[0:1, :] * full_value
        + taps_ref[1:2, :] * shift_down(full_value, halo, 1)
        + taps_ref[2:3, :] * shift_down(full_value, halo, 2)
    )
    sig = sigmoid(gate)
    passed = grad * gate * sig
    gate_grad = grad * convolved * sig * (1.0 + gate * (1.0 - sig))
    nothing = jnp.zeros((8, PAD), F32)
    value_grad = (
        value_grad
        + taps_ref[0:1, :] * passed
        + taps_ref[1:2, :] * shift_up(passed, nothing, 1)
        + taps_ref[2:3, :] * shift_up(passed, nothing, 2)
    )
    place = lanes(query_grad.shape)
    out_ref[:, :PAD] = jnp.where(place < HEAD, value_grad, query_grad).astype(BF)
    out_ref[:, PAD:] = jnp.where(place < HEAD, gate_grad, key_grad).astype(BF)


def back_later_kernel(
    block_ref, part_ref, keep_column_ref, later_ref, edge_ref, taps_ref,
    first_ref, second_ref, back_first_ref, back_second_ref, ones_ref, out_ref,
):
    block = block_ref[...]
    keep_column = keep_column_ref[...]
    right = block[:, PAD:]
    first = (nn(right, first_ref[...]) + ones_ref[0:1, :]) * keep_column
    second = nn(right, second_ref[...]) + ones_ref[1:2, :]
    second_kept = second * keep_column
    later = later_ref[0]
    value = halves(block)[0]
    feature_grad = nt(value, later)
    key_grad = nn((feature_grad * second_kept).astype(BF), back_first_ref[...]) + nn(
        (feature_grad * first).astype(BF), back_second_ref[...]
    )
    value_grad = nn((first * second).astype(BF), later)
    place = lanes(value_grad.shape)
    row = rows_of(value_grad.shape)
    count = block.shape[0]
    edge = edge_ref[...]
    last = taps_ref[1:2, :] * edge[0:1, :] + taps_ref[2:3, :] * edge[1:2, :]
    before_last = taps_ref[2:3, :] * edge[0:1, :]
    value_grad = value_grad + jnp.where(row == count - 1, last, jnp.where(row == count - 2, before_last, 0.0))
    part = part_ref[...].astype(F32)
    out_ref[:, :PAD] = (part[:, :PAD] + jnp.where(place < HEAD, value_grad, 0.0)).astype(BF)
    out_ref[:, PAD:] = (part[:, PAD:] + jnp.where(place < HEAD, 0.0, key_grad)).astype(BF)


def whole(shape):
    return pl.BlockSpec(shape, lambda *_: (0,) * len(shape))


def by_column(rows, width):
    return pl.BlockSpec((rows, width), lambda h: (0, h))


def by_head(shape):
    return pl.BlockSpec((1,) + shape, lambda h: (h, 0, 0))


def first_ffn_kernel(*refs):
    @pl.when(pl.program_id(0) == 0)
    def _():
        for ref in refs[12:15]:
            ref[...] = jnp.zeros_like(ref)

    ffn_body(*refs)


def later_ffn_kernel(*refs):
    @pl.when(pl.program_id(0) == 0)
    def _():
        for old, ref in zip(refs[12:15], refs[15:18]):
            ref[...] = old[...]

    ffn_body(*refs[:12], *refs[15:])


def ffn_body(
    normed_ref, top_ref, rank_ref, top_rank_ref, rank_turned_ref, top_rank_turned_ref,
    gate_ref, up_ref, down_ref, expand_gate_ref, expand_up_ref, reduce_ref,
    feed_ref, back_ref, small_ref, expand_gate_grad_ref, expand_up_grad_ref, reduce_grad_ref,
):
    normed = normed_ref[...]
    rank = rank_ref[...]
    width = normed.shape[1]
    gate, up, down = (r[...].reshape(-1, width) for r in (gate_ref, up_ref, down_ref))
    expand_gate, expand_up, reduce = expand_gate_ref[0], expand_up_ref[0], reduce_ref[0]
    gating = nt(normed, gate) + nn(rank, expand_gate)
    upward = nt(normed, up) + nn(rank, expand_up)
    hidden_grad = nt(top_ref[...], down) + nn(top_rank_ref[...], reduce)
    sig = sigmoid(gating)
    silu = gating * sig
    hidden = (silu * upward).astype(BF)
    up_grad = (hidden_grad * silu).astype(BF)
    gate_grad = (hidden_grad * upward * (sig + silu * (1.0 - sig))).astype(BF)
    feed_ref[...] += nn(hidden, down)
    back_ref[...] += nn(gate_grad, gate) + nn(up_grad, up)
    small_ref[0] += nt(hidden, reduce)
    small_ref[1] += nt(gate_grad, expand_gate) + nt(up_grad, expand_up)
    expand_gate_grad_ref[0] = nn(rank_turned_ref[...], gate_grad)
    expand_up_grad_ref[0] = nn(rank_turned_ref[...], up_grad)
    reduce_grad_ref[0] = nn(top_rank_turned_ref[...], hidden)


def ffn_part(normed, top, rank, top_rank, weights, weight_specs, tables, sums):
    rows, width = normed.shape
    ranks = rank.shape[1]
    steps, _, step = tables[0].shape
    once = pl.Buffered(1)

    def fixed(shape):
        return pl.BlockSpec(shape, lambda *_: (0,) * len(shape), pipeline_mode=once)

    by_step = pl.BlockSpec((1, ranks, step), lambda n: (n, 0, 0))
    return pl.pallas_call(
        later_ffn_kernel if sums else first_ffn_kernel,
        grid=(steps,),
        in_specs=[
            fixed((rows, width)), fixed((rows, width)), fixed((rows, ranks)), fixed((rows, ranks)),
            fixed((ranks, rows)), fixed((ranks, rows)),
            *weight_specs,
            by_step, by_step, by_step,
            *([fixed((rows, width)), fixed((rows, width)), fixed((2, rows, ranks))] if sums else []),
        ],
        out_specs=[
            fixed((rows, width)), fixed((rows, width)), fixed((2, rows, ranks)),
            by_step, by_step, by_step,
        ],
        out_shape=[
            jax.ShapeDtypeStruct((rows, width), F32),
            jax.ShapeDtypeStruct((rows, width), F32),
            jax.ShapeDtypeStruct((2, rows, ranks), F32),
        ]
        + [jax.ShapeDtypeStruct((steps, ranks, step), F32)] * 3,
        input_output_aliases={12: 0, 13: 1, 14: 2} if sums else {},
        name="ffn_part",
    )(normed, top, rank, top_rank, rank.T, top_rank.T, *weights, *tables, *sums)


def rms(values, gain):
    inverse = lax.rsqrt(jnp.mean(values * values, axis=-1, keepdims=True) + EPSILON)
    return values * inverse * gain


def rms_back(values, gain, upstream):
    inverse = lax.rsqrt(jnp.mean(values * values, axis=-1, keepdims=True) + EPSILON)
    scaled = upstream * gain
    mean = jnp.mean(values * scaled, axis=-1, keepdims=True)
    return inverse * scaled - values * (inverse * inverse * inverse) * mean


def dot(left, right, dims=((1,), (0,))):
    return lax.dot_general(left, right, (dims, ((), ())), preferred_element_type=F32)


ROWS = ((0,), (0,))
TURNED = ((1,), (1,))


def pad_heads(table):
    lead = table.shape[:-1]
    split = table.reshape(lead + (-1, HEAD))
    padded = jnp.pad(split, [(0, 0)] * len(lead) + [(0, 0), (0, PAD - HEAD)])
    return padded.reshape(lead + (-1,))


def unpad_heads(table):
    lead = table.shape[:-1]
    return table.reshape(lead + (-1, PAD))[..., :HEAD].reshape(lead + (-1,))


def after(value, *others):
    return lax.optimization_barrier((value,) + others)[0]


SWAP = [(0, 1), (1, 0)]


def on_device(
    tokens, cotangent, lengths, adapter_ids, gain_first, gain_second, conv_kernel, mixer_in, mixer_out, gate_up,
    down_weight, inward_down, inward_up, outward_down, outward_up, expand_down, expand_up, reduce_down, reduce_up,
):
    sequences, slot_rows, width = tokens.shape
    ways = lax.axis_size("wa")
    chips = lax.axis_size("g") * 4
    chip = lax.axis_index(CHIPS)
    core = lax.axis_index("c")
    place = lax.axis_index("wa")
    plane = lax.axis_index(PLANE)
    sequence = core * ways + place
    rows = slot_rows * sequences
    ranks = inward_down.shape[1]
    adapters = inward_down.shape[0]
    in_width = mixer_in.shape[1]
    out_here = mixer_out.shape[0]
    out_width = out_here // HEAD * PAD
    hidden_here = down_weight.shape[0]
    piece_rows = -(-hidden_here // 128) * 16
    hidden_gap = 8 * piece_rows - hidden_here
    gap_at = 7 * piece_rows
    slice_rows = width // 8
    next_place = [((d + 1) % ways, d) for d in range(ways)]
    last_place = [(d, (d + 1) % ways) for d in range(ways)]
    first, second, ones, order = constants()
    barrier = lax.optimization_barrier

    def reorder(columns):
        heads = range(0, columns.shape[1], PACK)
        return jnp.concatenate([dot(columns[:, h : h + PACK], order).astype(BF) for h in heads], axis=1)

    def from_next(piece):
        return lax.ppermute(piece, "wa", next_place)

    def from_last(piece):
        return lax.ppermute(piece, "wa", last_place)

    def plane_all(piece):
        return lax.all_gather(piece, PLANE, axis=0, tiled=True)

    def column_exchange(values):
        return lax.all_to_all(values, COLUMN, 0, 0, tiled=True).reshape(rows, width)

    own_in = reorder(lax.dynamic_slice_in_dim(mixer_in, plane * slice_rows, slice_rows, 0))
    own_out = pad_heads(lax.dynamic_slice_in_dim(mixer_out, plane * slice_rows, slice_rows, 1).T)
    mixer_slice = jnp.concatenate([own_in, own_out], axis=1)
    turned_gate_up = jnp.swapaxes(gate_up, 1, 2)
    start = jnp.minimum(plane * piece_rows, hidden_here - piece_rows)
    fresh = plane * piece_rows <= start + jnp.arange(piece_rows)
    gate_up_slice = lax.dynamic_slice(turned_gate_up, (0, start, 0), (2, piece_rows, width))
    down_slice = lax.dynamic_slice_in_dim(down_weight, start, piece_rows, 0)
    ffn_slice = jnp.concatenate([gate_up_slice.reshape(2 * piece_rows, width), down_slice], axis=0)
    ffn_slice = jnp.where(jnp.tile(fresh, 3)[:, None], ffn_slice, 0).astype(BF)

    own_tables = (inward_up, outward_down, expand_up.reshape(adapters, ranks, -1), reduce_down)

    def tables_for(target):
        which = adapter_ids[target]
        return jnp.concatenate(
            [lax.dynamic_index_in_dim(t, which, 0, keepdims=False) for t in own_tables], axis=1
        )

    prepared = [tables_for(sequence)]
    for j in range(1, ways):
        prepared.append(tables_for(core * ways + (place - j) % ways))
    held = barrier((from_next(mixer_slice), mixer_slice, ffn_slice) + tuple(prepared))
    (mixer_1, mixer_slice, ffn_slice), prepared = held[:3], held[3:]
    mixer_2, mixer_3 = from_next(mixer_1), from_last(mixer_slice)
    gathered_near = plane_all(mixer_1)
    tables = [prepared[0]]
    for j in range(1, ways):
        pairs = [(s, (s - j) % ways) for s in range(ways)]
        tables.append(lax.ppermute(prepared[j], "wa", pairs))
    held = barrier((mixer_2, mixer_3, ffn_slice, pad_heads(mixer_out.T)) + tuple(tables[1:]))
    (mixer_2, mixer_3, ffn_slice, out_own), tables[1:] = held[:4], held[4:]
    gathered_rest = plane_all(
        jnp.concatenate(
            [mixer_2[:, :in_width], mixer_3[:, :in_width], mixer_2[:, in_width:], mixer_3[:, in_width:]], axis=1
        )
    )
    cut = [in_width, out_here, hidden_here, hidden_here, hidden_here]
    edges = np.cumsum([0] + cut)
    split_tables = [[t[:, edges[n] : edges[n + 1]] for n in range(5)] for t in tables]
    inward_second = reorder(jnp.concatenate([t[0] for t in split_tables], axis=1))
    outward_first = jnp.concatenate([pad_heads(t[1]) for t in split_tables], axis=1)
    ffn_1, tokens_in, in_own = barrier((from_next(ffn_slice), tokens, reorder(mixer_in)))
    gathered_1 = plane_all(ffn_1)
    in_split = (ways - 2) * in_width
    in_weights = jnp.concatenate([in_own, gathered_near[:, :in_width], gathered_rest[:, :in_split]], axis=1)
    out_weights = jnp.concatenate([out_own, gathered_near[:, in_width:], gathered_rest[:, in_split:]], axis=1)
    x, ffn_slice, in_weights, out_weights, inward_second = barrier(
        (column_exchange(tokens_in), ffn_slice, in_weights, out_weights, inward_second)
    )
    ffn_tables = []
    for j in range(ways):
        chosen = jnp.stack(split_tables[j][2:5])
        if j > 0:
            empty = jnp.zeros((3, ranks, hidden_gap), BF)
            chosen = jnp.concatenate([chosen[..., :gap_at], empty, chosen[..., gap_at:]], axis=2)
        ffn_tables.append(jnp.swapaxes(chosen.reshape(3, ranks, 2, -1), 1, 2))
    ffn_3 = from_last(ffn_slice)

    which = adapter_ids[sequence]

    def pick(table):
        return lax.dynamic_index_in_dim(table, which, 0, keepdims=False)

    inward_first, outward_second = pick(inward_down), pick(outward_up)
    expand_first, reduce_second = pick(expand_down), pick(reduce_up)
    positions = chip * rows + jnp.arange(rows, dtype=jnp.int32)
    keep = (positions < lengths[sequence]).astype(F32)
    keep_row, keep_column = keep[None, :], keep[:, None]

    inputs = x.astype(F32)
    normed = rms(inputs, gain_first).astype(BF)
    enter = dot(normed, inward_first, TURNED).astype(BF)
    packed = (dot(normed, in_weights) + dot(enter, inward_second)).astype(BF)
    taps = pad_heads(jnp.roll(conv_kernel.astype(F32), -place * out_here, axis=1))
    taps = jnp.pad(taps, ((0, 5), (0, 0)))

    def chip_shift(piece, by):
        pairs = [(i, i + by) for i in range(chips) if 0 <= i + by < chips]
        return lax.ppermute(piece, CHIPS, pairs)


    def flip(piece, bit, keep_pair=lambda i: True):
        return lax.ppermute(piece, CHIPS, [(i, i ^ bit) for i in range(chips) if keep_pair(i)])

    def scan_chips(local, sent, want_bit, ahead):
        before = jnp.zeros_like(local)
        total = local
        bit = 1
        while bit < chips:
            if bit > 1:
                sent = total.astype(BF)
            if bit == 2:
                sent = ahead(sent)
            last = 2 * bit >= chips
            got = flip(sent, bit, lambda i: not last or ((i & bit) == 0) == want_bit).astype(F32)
            take = ((chip & bit) != 0) == want_bit
            before = before + jnp.where(take, got, 0.0)
            total = total + got
            bit *= 2
        return before.astype(BF)

    pairs_shape = (PAIRS, PAD)
    ones_column = ones.T
    head_params = pltpu.CompilerParams(dimension_semantics=("arbitrary",))
    packed_spec, head_spec = by_column(rows, PACK), by_column(rows, PAD)
    halo_spec, edge_spec, state_spec = by_column(8, PACK), by_column(8, PAD), by_head(pairs_shape)
    turn_specs = [whole((PAIRS, PAD)), whole((PAIRS, PAD)), whole((PAIRS, 3))]
    pick_specs = [whole((PAD, PAIRS)), whole((PAD, PAIRS))]
    back_specs = [whole((PAIRS, PAD)), whole((PAIRS, PAD)), whole((3, PAIRS))]
    narrow = jax.ShapeDtypeStruct((rows, HEADS * PAD), BF)
    packed_shape = jax.ShapeDtypeStruct((rows, HEADS * PACK), BF)
    state_shape = jax.ShapeDtypeStruct((HEADS,) + pairs_shape, F32)

    state = pl.pallas_call(
        state_kernel,
        grid=(HEADS,),
        in_specs=[packed_spec, whole((1, rows))] + turn_specs,
        out_specs=state_spec,
        out_shape=state_shape,
        compiler_params=head_params,
        name="state",
    )(packed, keep_row, first.T, second.T, ones_column)
    state_sent, last_rows = barrier((state.astype(BF), packed[-8:]))
    ffn_3, cot_in, halo = barrier((ffn_3, cotangent, chip_shift(last_rows, 1)))
    gathered_3 = plane_all(ffn_3)
    cot = column_exchange(cot_in)
    before = scan_chips(state, state_sent, True, lambda sent: sent)
    staged = []
    inside = pl.pallas_call(
        inside_kernel,
        grid=(HEADS,),
        in_specs=[packed_spec, whole((rows, 1))],
        out_specs=head_spec,
        out_shape=jax.ShapeDtypeStruct((rows, HEADS * PAD), F32),
        compiler_params=head_params,
        name="inside",
    )(packed, keep_column)
    held = barrier((ffn_1, cot, inside, before, outward_first) + tuple(ffn_tables))
    (ffn_1, cot, inside, before, outward_first), ffn_tables = held[:5], held[5:]
    ffn_2 = from_next(ffn_1)
    mixed, kept = pl.pallas_call(
        mixer_kernel,
        grid=(HEADS,),
        in_specs=[packed_spec, head_spec, state_spec, halo_spec, edge_spec] + pick_specs + [whole((3, PAIRS))],
        out_specs=[head_spec, head_spec],
        out_shape=[narrow, narrow],
        compiler_params=head_params,
        name="mixer",
    )(packed, inside, before, halo, taps, first, second, ones)

    leave = dot(mixed, outward_first, TURNED).astype(BF)
    residual = inputs + dot(mixed, out_weights, TURNED) + dot(leave, outward_second)
    normed_two = rms(residual, gain_second).astype(BF)
    top = jnp.where(keep_column > 0, cot, jnp.zeros_like(cot))
    top_rank = dot(top, reduce_second, TURNED).astype(BF)
    normed_two, ffn_2, top, top_rank = barrier((normed_two, ffn_2, top, top_rank))
    gathered_far = plane_all(ffn_2)
    expand = dot(normed_two, expand_first, TURNED).astype(BF)

    def own_spec(which):
        return pl.BlockSpec((1, hidden_here // 2, width), lambda n: (which, n, 0))

    def piece_spec(which):
        return pl.BlockSpec((4, 1, piece_rows, width), lambda n: (n, which, 0, 0))

    specs_for = [piece_spec(t) for t in range(3)]

    def parts_of(gathered):
        return (gathered.reshape(8, 3, piece_rows, width),) * 3

    plans = [
        (0, (turned_gate_up, turned_gate_up, down_weight[None]), [own_spec(0), own_spec(1), own_spec(0)]),
        (1, parts_of(gathered_1), specs_for),
        (3, parts_of(gathered_3), specs_for),
        (2, parts_of(gathered_far), specs_for),
    ]
    expand_grads, sums = [None] * ways, ()
    for j, weights, specs in plans:
        *sums, g_gate, g_up, g_reduce = ffn_part(normed_two, top, expand, top_rank, weights, specs, ffn_tables[j], tuple(sums))
        sums, grads = tuple(sums), (g_gate, g_up, g_reduce)
        grads = jnp.swapaxes(jnp.stack(grads), 1, 2).reshape(3, ranks, -1)
        if j > 0:
            grads = jnp.concatenate([grads[..., :gap_at], grads[..., gap_at + hidden_gap :]], axis=2)
        expand_grads[j] = [grads[0], grads[1], grads[2]]
    feed, back, small = sums
    reduce_rank = small[0].astype(BF)
    expand_grad = small[1].astype(BF)
    back = back + dot(expand_grad, expand_first)
    grad_reduce_up = dot(reduce_rank, top, ROWS)
    grad_expand_down = dot(expand_grad, normed_two, ROWS)
    residual_grad = top.astype(F32) + rms_back(residual, gain_second, back)
    branch = residual_grad.astype(BF)
    leave_grad = dot(branch, outward_second, TURNED).astype(BF)
    grad_outward_up = dot(leave, branch, ROWS)
    mixed_grad = (dot(branch, out_weights) + dot(leave_grad, outward_first)).astype(BF)
    grad_outward_down = unpad_heads(dot(leave_grad, mixed, ROWS))

    scaled, back_state, edge = pl.pallas_call(
        back_state_kernel,
        grid=(HEADS,),
        in_specs=[packed_spec, head_spec, head_spec] + turn_specs,
        out_specs=[head_spec, state_spec, edge_spec],
        out_shape=[narrow, state_shape, jax.ShapeDtypeStruct((8, HEADS * PAD), F32)],
        compiler_params=head_params,
        name="back_state",
    )(packed, kept, mixed_grad, first.T, second.T, ones_column)
    hot = (jnp.arange(adapters, dtype=jnp.int32)[:, None] == adapter_ids[None, :]).astype(F32)
    hot = hot.reshape(adapters, 2, ways)
    hot = jnp.where(core == 0, hot, hot[:, ::-1])
    turned = [lax.dynamic_index_in_dim(hot, (place - j) % ways, 2, keepdims=False) for j in range(ways)]
    turned = [lax.dynamic_index_in_dim(jnp.stack(turned, axis=2), (chip % 4) ^ k, 2, keepdims=False) for k in range(4)]
    hot = jnp.stack(turned, axis=2).reshape(adapters, 8)
    same_rank = jnp.eye(ranks, dtype=F32)[None, :, None, :]
    hot_rows = (hot[:, None, :, None] * same_rank).reshape(adapters * ranks, 8 * ranks).astype(BF)

    def exchange_places(pieces):
        got = [pieces(0).astype(BF)]
        for j in range(1, ways):
            pairs = [(s, (s + j) % ways) for s in range(ways)]
            got.append(lax.ppermute(pieces(j).astype(BF), "wa", pairs))
        return jnp.stack(got)

    def exchange_chips(table):
        bit = 4
        while bit < chips:
            table = (table.astype(F32) + flip(table, bit).astype(F32)).astype(BF)
            bit *= 2

        def sequence_at(other):
            return lax.dynamic_index_in_dim(table, (chip % 4) ^ other, 0, keepdims=False)

        summed = sum([flip(sequence_at(k), k).astype(F32) for k in range(1, 4)], sequence_at(0).astype(F32)).astype(BF)
        parts = jnp.concatenate([summed] + [flip(summed, k) for k in range(1, 4)], axis=0)
        parts = jnp.concatenate([parts, lax.ppermute(parts, "c", SWAP)], axis=0)
        return dot(hot_rows, parts).reshape(adapters, ranks, -1)

    shard = width // ways

    def shard_of(table, j):
        return lax.dynamic_slice_in_dim(table, (place + j) % ways * shard, shard, 1)

    any_space = pl.BlockSpec(memory_space=pl.ANY)

    def back_inside(base, scaled, old):
        def shift(spec):
            return pl.BlockSpec(spec.block_shape, lambda h, m=spec.index_map: m(h + base))

        return pl.pallas_call(
            back_inside_kernel if old is None else lambda *refs: back_inside_kernel(*refs[:12], refs[-1]),
            grid=(HEADS // 2,),
            in_specs=[
                shift(packed_spec), shift(head_spec), shift(head_spec), whole((rows, 1)),
                shift(state_spec), shift(halo_spec), shift(edge_spec),
            ]
            + pick_specs
            + back_specs
            + ([] if old is None else [any_space]),
            out_specs=shift(packed_spec),
            out_shape=packed_shape,
            input_output_aliases={} if old is None else {12: 0},
            compiler_params=head_params,
            name="back_inside",
        )(
            packed, scaled, mixed_grad, keep_column, before, halo, taps, first, second, first.T, second.T, ones,
            *(() if old is None else (old,)),
        )

    def inside_first(sent):
        sent, part, again, *rest = barrier((sent, back_inside(0, scaled, None), scaled, feed) + outer_grads)
        staged.append((back_inside(HEADS // 2, again, part), rest))
        return sent

    outer_grads = (grad_outward_down, grad_outward_up, grad_expand_down, grad_reduce_up)
    edge = chip_shift(edge, -1)
    later = scan_chips(back_state, back_state.astype(BF), False, inside_first)
    part, (feed, *outer_grads) = staged[0]
    output = (keep_column * (residual + feed + dot(reduce_rank, reduce_second))).astype(BF)

    def send_back(values):
        return lax.all_to_all(values.reshape(sequences, slot_rows, -1), COLUMN, 0, 0, tiled=True)

    packed_grad = pl.pallas_call(
        back_later_kernel,
        grid=(HEADS,),
        in_specs=[packed_spec, packed_spec, whole((rows, 1)), state_spec, edge_spec, edge_spec]
        + pick_specs
        + back_specs,
        out_specs=packed_spec,
        out_shape=packed_shape,
        compiler_params=head_params,
        name="back_later",
    )(packed, part, keep_column, later, edge, taps, first, second, first.T, second.T, ones)

    packed_grad, back_first = barrier((packed_grad, send_back(output[:, : width // 2])))
    back_last = send_back(after(output[:, width // 2 :], back_first))
    enter_grad = dot(packed_grad, inward_second, TURNED).astype(BF)
    normed_grad = (
        dot(packed_grad, in_weights, TURNED) + dot(enter_grad, inward_first)
    )
    input_grad = (branch.astype(F32) + rms_back(inputs, gain_first, normed_grad)).astype(BF)
    input_grad, back_last, late_grad, late_enter = barrier((input_grad, back_last, packed_grad, enter_grad))
    third = -(-width // 384) * 128
    input_first = send_back(input_grad[:, :third])
    input_next = send_back(after(input_grad[:, third : 2 * third], input_first))
    input_last = send_back(after(input_grad[:, 2 * third :], input_next))
    late_grad, late_enter = barrier((late_grad, late_enter, input_first))[:2]
    grad_inward_up = dot(dot(enter, late_grad, ROWS).astype(BF).reshape(-1, PACK), order, TURNED).astype(BF)
    grad_inward_up = grad_inward_up.reshape(ranks, -1)
    grad_inward_down = dot(late_enter, normed, ROWS)

    places = exchange_places(
        lambda j: jnp.concatenate(
            expand_grads[j]
            + [outer_grads[0][:, j * out_here : (j + 1) * out_here]]
            + [shard_of(t, j) for t in outer_grads[1:]]
            + [grad_inward_up[:, j * in_width : (j + 1) * in_width], shard_of(grad_inward_down, j)],
            axis=1,
        )
    )
    sums = exchange_chips(after(places, input_next))
    at = np.cumsum([0, 2 * hidden_here, hidden_here, out_here, shard, shard, shard, in_width, shard])
    grads = [sums[:, :, at[n] : at[n + 1]] for n in range(8)]
    return (
        jnp.concatenate([back_first, back_last], axis=2).astype(F32),
        jnp.concatenate([input_first, input_next, input_last], axis=2).astype(F32),
        grads[7],
        grads[6],
        grads[2],
        grads[3],
        grads[4],
        grads[0].reshape(adapters, ranks, 2, hidden_here),
        grads[1],
        grads[5],
    )


def solution(mesh):
    ways = mesh.shape["wa"]
    split = Mesh(mesh.devices.reshape(-1, 2, 2, 2, ways), EVERY)
    slots = P(None, EVERY, None)
    in_specs = (
        slots, slots, P(), P(), P(), P(), P(),
        P(None, "wa"), P("wa", None), P(None, None, "wa"), P("wa", None),
        P(), P(None, None, "wa"), P(None, None, "wa"), P(), P(), P(None, None, None, "wa"), P(None, None, "wa"), P(),
    )
    third = P(None, None, "wa")
    out_specs = (slots, slots, third, third, third, third, third, P(None, None, None, "wa"), third, third)
    return jax.shard_map(on_device, mesh=split, in_specs=in_specs, out_specs=out_specs, check_vma=False)
```

```python
import math

import jax
import jax.numpy as jnp
import numpy as np
from jax import lax
from jax.experimental import pallas as pl
from jax.experimental.pallas import tpu as pltpu
from jax.sharding import Mesh
from jax.sharding import PartitionSpec as P

HEADS = 16
HEAD = 112
FEAT = 16
PACK = 256
PAD = 128
PAIRS = 160
ONE_LANE = HEAD

EPSILON = 1e-05
BF = jnp.bfloat16
F32 = jnp.float32

CHIPS = ("g", "b", "a")
PLANE = ("b", "a", "c")
COLUMN = ("c", "wa")
EVERY = ("g", "b", "a", "c", "wa")


def constants():
    pairs = [(i, j) for i in range(FEAT + 1) for j in range(i, FEAT + 1)]
    first = np.zeros((PAD, PAIRS), np.float32)
    second = np.zeros((PAD, PAIRS), np.float32)
    ones = np.zeros((3, PAIRS), np.float32)
    for f, (i, j) in enumerate(pairs):
        if i > 0:
            first[HEAD + i - 1, f] = 0.5
        if j > 0:
            second[HEAD + j - 1, f] = 0.5
        ones[0, f] = 1.0 if i == 0 else 0.0
        ones[1, f] = 1.0 if j == 0 else 0.0
        ones[2, f] = 0.5 if i == j and i > 0 else 1.0
    order = np.zeros((PACK, PACK), np.float32)
    for i in range(FEAT):
        order[i, HEAD + i] = 1.0
        order[FEAT + i, PAD + HEAD + i] = 1.0
    for i in range(HEAD):
        order[2 * FEAT + i, i] = 1.0
        order[2 * FEAT + HEAD + i, PAD + i] = 1.0
    return jnp.asarray(first, BF), jnp.asarray(second, BF), jnp.asarray(ones), jnp.asarray(order, BF)


def nn(left, right):
    return lax.dot_general(left, right, (((1,), (0,)), ((), ())), preferred_element_type=F32)


def nt(left, right):
    return lax.dot_general(left, right, (((1,), (1,)), ((), ())), preferred_element_type=F32)


def lanes(shape):
    return lax.broadcasted_iota(jnp.int32, shape, 1)


def rows_of(shape):
    return lax.broadcasted_iota(jnp.int32, shape, 0)


def tn(left, right):
    return lax.dot_general(left, right, (((0,), (0,)), ((), ())), preferred_element_type=F32)


def halves(block):
    left, right = block[:, :PAD], block[:, PAD:]
    place = lanes(left.shape)
    zero = jnp.zeros_like(left)
    value = jnp.where(place < HEAD, left, jnp.where(place == ONE_LANE, jnp.ones_like(left), zero))
    query = jnp.where(place < HEAD, zero, left)
    gate = jnp.where(place < HEAD, right, zero)
    key = jnp.where(place < HEAD, zero, right)
    return value, query, gate, key


def shift_down(values, halo, by):
    rolled = pltpu.roll(values, by, 0)
    place = rows_of(values.shape)
    for row in range(by):
        rolled = jnp.where(place == row, halo[8 - by + row : 9 - by + row, :], rolled)
    return rolled


def shift_up(values, halo, by):
    count = values.shape[0]
    rolled = pltpu.roll(values, count - by, 0)
    place = rows_of(values.shape)
    for row in range(by):
        rolled = jnp.where(place == count - by + row, halo[row : row + 1, :], rolled)
    return rolled


def sigmoid(values):
    return 1.0 / (1.0 + jnp.exp(-values))


def state_kernel(block_ref, keep_ref, first_ref, second_ref, ones_ref, out_ref):
    block = block_ref[...]
    right = block[:, PAD:]
    first = nt(first_ref[...], right) + ones_ref[:, 0:1]
    second = nt(second_ref[...], right) + ones_ref[:, 1:2]
    features = (first * second * keep_ref[...]).astype(BF)
    out_ref[0] = nn(features, halves(block)[0])


def inside_kernel(block_ref, keep_column_ref, out_ref):
    value, query, _, key = halves(block_ref[...])
    half = value.shape[0] // 2
    value = value * keep_column_ref[...].astype(BF)
    key = key * 0.25
    causal = rows_of((half, half)) >= lanes((half, half))
    for r in range(2):
        total = 0.0
        for c in range(r + 1):
            score = 1.0 + nt(query[r * half : (r + 1) * half], key[c * half : (c + 1) * half])
            weight = 0.5 * score * score + 0.5
            if r == c:
                weight = jnp.where(causal, weight, 0.0)
            total = total + nn(weight.astype(BF), value[c * half : (c + 1) * half])
        out_ref[r * half : (r + 1) * half, :] = total


def mixer_kernel(
    block_ref, inside_ref, state_ref, halo_ref, taps_ref, first_ref, second_ref, ones_ref, mixed_ref, kept_ref
):
    block = block_ref[...]
    left = block[:, :PAD]
    first = nn(left, first_ref[...]) + ones_ref[0:1, :]
    second = nn(left, second_ref[...]) + ones_ref[1:2, :]
    features = (first * second * ones_ref[2:3, :]).astype(BF)
    value, _, gate, _ = halves(block)
    value, gate = value.astype(F32), gate.astype(F32)
    total = inside_ref[...] + nn(features, state_ref[0])
    inverse = 1.0 / total[:, ONE_LANE : ONE_LANE + 1]
    attended = total * inverse
    halo = halo_ref[:, :PAD].astype(F32)
    convolved = (
        taps_ref[0:1, :] * value
        + taps_ref[1:2, :] * shift_down(value, halo, 1)
        + taps_ref[2:3, :] * shift_down(value, halo, 2)
    )
    mixed = attended + convolved * gate * sigmoid(gate)
    place = lanes(mixed.shape)
    mixed_ref[...] = jnp.where(place < HEAD, mixed, 0.0).astype(BF)
    kept_ref[...] = jnp.where(
        place < HEAD, attended, jnp.where(place == ONE_LANE, inverse, 0.0)
    ).astype(BF)


def back_state_kernel(
    block_ref, kept_ref, grad_ref, first_ref, second_ref, ones_ref, scaled_ref, state_ref, edge_ref
):
    block = block_ref[...]
    grad = grad_ref[...].astype(F32)
    kept = kept_ref[...].astype(F32)
    place = lanes(grad.shape)
    inverse = kept[:, ONE_LANE : ONE_LANE + 1]
    along = jnp.sum(grad * kept, axis=1, keepdims=True)
    scaled = (jnp.where(place == ONE_LANE, -along, grad) * inverse).astype(BF)
    scaled_ref[...] = scaled
    left = block[:, :PAD]
    first = nt(first_ref[...], left) + ones_ref[:, 0:1]
    second = nt(second_ref[...], left) + ones_ref[:, 1:2]
    features = (first * second * ones_ref[:, 2:3]).astype(BF)
    state_ref[0] = nn(features, scaled)
    gate = block[:8, PAD:].astype(F32)
    edge_ref[...] = grad[:8] * gate * sigmoid(gate)


def back_inside_kernel(
    block_ref, scaled_ref, grad_ref, keep_column_ref, state_ref, halo_ref, taps_ref,
    first_ref, second_ref, back_first_ref, back_second_ref, ones_ref, out_ref,
):
    block = block_ref[...]
    rows = block.shape[0]
    half = rows // 2
    scaled = scaled_ref[...]
    grad = grad_ref[...].astype(F32)
    keep_column = keep_column_ref[...]
    value, query, gate, key = halves(block)
    full_value, gate = value.astype(F32), gate.astype(F32)
    value = value * keep_column.astype(BF)
    left = block[:, :PAD]
    first = (nn(left, first_ref[...]) + ones_ref[0:1, :]) * ones_ref[2:3, :]
    second = (nn(left, second_ref[...]) + ones_ref[1:2, :]) * ones_ref[2:3, :]
    feature_grad = nt(scaled, state_ref[0])
    query_grad = nn((feature_grad * second).astype(BF), back_first_ref[...]) + nn(
        (feature_grad * first).astype(BF), back_second_ref[...]
    )
    key = key * 0.25
    query_after = query * 0.25
    causal = rows_of((half, half)) >= lanes((half, half))
    query_sums = []
    key_sums = [0.0, 0.0]
    value_sums = [0.0, 0.0]
    for r in range(2):
        here_r = slice(r * half, (r + 1) * half)
        query_sum = query_grad[here_r]
        for c in range(r + 1):
            here_c = slice(c * half, (c + 1) * half)
            score = 1.0 + nt(query[here_r], key[here_c])
            score_grad = score * nt(scaled[here_r], value[here_c])
            weight = 0.5 * score * score + 0.5
            if r == c:
                score_grad = jnp.where(causal, score_grad, 0.0)
                weight = jnp.where(causal, weight, 0.0)
            score_grad = score_grad.astype(BF)
            query_sum = query_sum + nn(score_grad, key[here_c])
            key_sums[c] = key_sums[c] + tn(score_grad, query_after[here_r])
            value_sums[c] = value_sums[c] + tn(weight.astype(BF), scaled[here_r])
        query_sums.append(query_sum)
    query_grad = jnp.concatenate(query_sums, axis=0)
    key_grad = jnp.concatenate(key_sums, axis=0)
    value_grad = jnp.concatenate(value_sums, axis=0) * keep_column
    halo = halo_ref[:, :PAD].astype(F32)
    convolved = (
        taps_ref[0:1, :] * full_value
        + taps_ref[1:2, :] * shift_down(full_value, halo, 1)
        + taps_ref[2:3, :] * shift_down(full_value, halo, 2)
    )
    sig = sigmoid(gate)
    passed = grad * gate * sig
    gate_grad = grad * convolved * sig * (1.0 + gate * (1.0 - sig))
    nothing = jnp.zeros((8, PAD), F32)
    value_grad = (
        value_grad
        + taps_ref[0:1, :] * passed
        + taps_ref[1:2, :] * shift_up(passed, nothing, 1)
        + taps_ref[2:3, :] * shift_up(passed, nothing, 2)
    )
    place = lanes(query_grad.shape)
    out_ref[:, :PAD] = jnp.where(place < HEAD, value_grad, query_grad).astype(BF)
    out_ref[:, PAD:] = jnp.where(place < HEAD, gate_grad, key_grad).astype(BF)


def back_later_kernel(
    block_ref, part_ref, keep_column_ref, later_ref, edge_ref, taps_ref,
    first_ref, second_ref, back_first_ref, back_second_ref, ones_ref, out_ref,
):
    block = block_ref[...]
    keep_column = keep_column_ref[...]
    right = block[:, PAD:]
    first = (nn(right, first_ref[...]) + ones_ref[0:1, :]) * keep_column
    second = nn(right, second_ref[...]) + ones_ref[1:2, :]
    second_kept = second * keep_column
    later = later_ref[0]
    value = halves(block)[0]
    feature_grad = nt(value, later)
    key_grad = nn((feature_grad * second_kept).astype(BF), back_first_ref[...]) + nn(
        (feature_grad * first).astype(BF), back_second_ref[...]
    )
    value_grad = nn((first * second).astype(BF), later)
    place = lanes(value_grad.shape)
    row = rows_of(value_grad.shape)
    count = block.shape[0]
    edge = edge_ref[...]
    last = taps_ref[1:2, :] * edge[0:1, :] + taps_ref[2:3, :] * edge[1:2, :]
    before_last = taps_ref[2:3, :] * edge[0:1, :]
    value_grad = value_grad + jnp.where(row == count - 1, last, jnp.where(row == count - 2, before_last, 0.0))
    part = part_ref[...].astype(F32)
    out_ref[:, :PAD] = (part[:, :PAD] + jnp.where(place < HEAD, value_grad, 0.0)).astype(BF)
    out_ref[:, PAD:] = (part[:, PAD:] + jnp.where(place < HEAD, 0.0, key_grad)).astype(BF)


def whole(shape):
    return pl.BlockSpec(shape, lambda *_: (0,) * len(shape))


def by_column(rows, width):
    return pl.BlockSpec((rows, width), lambda h: (0, h))


def by_head(shape):
    return pl.BlockSpec((1,) + shape, lambda h: (h, 0, 0))


def first_ffn_kernel(*refs):
    @pl.when(pl.program_id(0) == 0)
    def _():
        for ref in refs[12:15]:
            ref[...] = jnp.zeros_like(ref)

    ffn_body(*refs)


def later_ffn_kernel(*refs):
    @pl.when(pl.program_id(0) == 0)
    def _():
        for old, ref in zip(refs[12:15], refs[15:18]):
            ref[...] = old[...]

    ffn_body(*refs[:12], *refs[15:])


def ffn_body(
    normed_ref, top_ref, rank_ref, top_rank_ref, rank_turned_ref, top_rank_turned_ref,
    gate_ref, up_ref, down_ref, expand_gate_ref, expand_up_ref, reduce_ref,
    feed_ref, back_ref, small_ref, expand_gate_grad_ref, expand_up_grad_ref, reduce_grad_ref,
):
    normed = normed_ref[...]
    rank = rank_ref[...]
    width = normed.shape[1]
    gate, up, down = (r[...].reshape(-1, width) for r in (gate_ref, up_ref, down_ref))
    expand_gate, expand_up, reduce = expand_gate_ref[0], expand_up_ref[0], reduce_ref[0]
    gating = nt(normed, gate) + nn(rank, expand_gate)
    upward = nt(normed, up) + nn(rank, expand_up)
    hidden_grad = nt(top_ref[...], down) + nn(top_rank_ref[...], reduce)
    sig = sigmoid(gating)
    silu = gating * sig
    hidden = (silu * upward).astype(BF)
    up_grad = (hidden_grad * silu).astype(BF)
    gate_grad = (hidden_grad * upward * (sig + silu * (1.0 - sig))).astype(BF)
    feed_ref[...] += nn(hidden, down)
    back_ref[...] += nn(gate_grad, gate) + nn(up_grad, up)
    small_ref[0] += nt(hidden, reduce)
    small_ref[1] += nt(gate_grad, expand_gate) + nt(up_grad, expand_up)
    expand_gate_grad_ref[0] = nn(rank_turned_ref[...], gate_grad)
    expand_up_grad_ref[0] = nn(rank_turned_ref[...], up_grad)
    reduce_grad_ref[0] = nn(top_rank_turned_ref[...], hidden)


def ffn_part(normed, top, rank, top_rank, weights, weight_specs, tables, sums):
    rows, width = normed.shape
    ranks = rank.shape[1]
    steps, _, step = tables[0].shape
    once = pl.Buffered(1)

    def fixed(shape):
        return pl.BlockSpec(shape, lambda *_: (0,) * len(shape), pipeline_mode=once)

    by_step = pl.BlockSpec((1, ranks, step), lambda n: (n, 0, 0))
    return pl.pallas_call(
        later_ffn_kernel if sums else first_ffn_kernel,
        grid=(steps,),
        in_specs=[
            fixed((rows, width)), fixed((rows, width)), fixed((rows, ranks)), fixed((rows, ranks)),
            fixed((ranks, rows)), fixed((ranks, rows)),
            *weight_specs,
            by_step, by_step, by_step,
            *([fixed((rows, width)), fixed((rows, width)), fixed((2, rows, ranks))] if sums else []),
        ],
        out_specs=[
            fixed((rows, width)), fixed((rows, width)), fixed((2, rows, ranks)),
            by_step, by_step, by_step,
        ],
        out_shape=[
            jax.ShapeDtypeStruct((rows, width), F32),
            jax.ShapeDtypeStruct((rows, width), F32),
            jax.ShapeDtypeStruct((2, rows, ranks), F32),
        ]
        + [jax.ShapeDtypeStruct((steps, ranks, step), F32)] * 3,
        input_output_aliases={12: 0, 13: 1, 14: 2} if sums else {},
        name="ffn_part",
    )(normed, top, rank, top_rank, rank.T, top_rank.T, *weights, *tables, *sums)


def rms(values, gain):
    inverse = lax.rsqrt(jnp.mean(values * values, axis=-1, keepdims=True) + EPSILON)
    return values * inverse * gain


def rms_back(values, gain, upstream):
    inverse = lax.rsqrt(jnp.mean(values * values, axis=-1, keepdims=True) + EPSILON)
    scaled = upstream * gain
    mean = jnp.mean(values * scaled, axis=-1, keepdims=True)
    return inverse * scaled - values * (inverse * inverse * inverse) * mean


def dot(left, right, dims=((1,), (0,))):
    return lax.dot_general(left, right, (dims, ((), ())), preferred_element_type=F32)


ROWS = ((0,), (0,))
TURNED = ((1,), (1,))


def pad_heads(table):
    lead = table.shape[:-1]
    split = table.reshape(lead + (-1, HEAD))
    padded = jnp.pad(split, [(0, 0)] * len(lead) + [(0, 0), (0, PAD - HEAD)])
    return padded.reshape(lead + (-1,))


def unpad_heads(table):
    lead = table.shape[:-1]
    return table.reshape(lead + (-1, PAD))[..., :HEAD].reshape(lead + (-1,))


def after(value, *others):
    return lax.optimization_barrier((value,) + others)[0]


SWAP = [(0, 1), (1, 0)]


def on_device(
    tokens, cotangent, lengths, adapter_ids, gain_first, gain_second, conv_kernel, mixer_in, mixer_out, gate_up,
    down_weight, inward_down, inward_up, outward_down, outward_up, expand_down, expand_up, reduce_down, reduce_up,
):
    sequences, slot_rows, width = tokens.shape
    ways = lax.axis_size("wa")
    chips = lax.axis_size("g") * 4
    chip = lax.axis_index(CHIPS)
    core = lax.axis_index("c")
    place = lax.axis_index("wa")
    plane = lax.axis_index(PLANE)
    sequence = core * ways + place
    rows = slot_rows * sequences
    ranks = inward_down.shape[1]
    adapters = inward_down.shape[0]
    in_width = mixer_in.shape[1]
    out_here = mixer_out.shape[0]
    out_width = out_here // HEAD * PAD
    hidden_here = down_weight.shape[0]
    piece_rows = -(-hidden_here // 128) * 16
    hidden_gap = 8 * piece_rows - hidden_here
    gap_at = 7 * piece_rows
    slice_rows = width // 8
    next_place = [((d + 1) % ways, d) for d in range(ways)]
    last_place = [(d, (d + 1) % ways) for d in range(ways)]
    first, second, ones, order = constants()
    barrier = lax.optimization_barrier

    def reorder(columns):
        heads = range(0, columns.shape[1], PACK)
        return jnp.concatenate([dot(columns[:, h : h + PACK], order).astype(BF) for h in heads], axis=1)

    def from_next(piece):
        return lax.ppermute(piece, "wa", next_place)

    def from_last(piece):
        return lax.ppermute(piece, "wa", last_place)

    def plane_all(piece):
        return lax.all_gather(piece, PLANE, axis=0, tiled=True)

    def column_exchange(values):
        return lax.all_to_all(values, COLUMN, 0, 0, tiled=True).reshape(rows, width)

    own_in = reorder(lax.dynamic_slice_in_dim(mixer_in, plane * slice_rows, slice_rows, 0))
    own_out = pad_heads(lax.dynamic_slice_in_dim(mixer_out, plane * slice_rows, slice_rows, 1).T)
    mixer_slice = jnp.concatenate([own_in, own_out], axis=1)
    turned_gate_up = jnp.swapaxes(gate_up, 1, 2)
    start = jnp.minimum(plane * piece_rows, hidden_here - piece_rows)
    fresh = plane * piece_rows <= start + jnp.arange(piece_rows)
    gate_up_slice = lax.dynamic_slice(turned_gate_up, (0, start, 0), (2, piece_rows, width))
    down_slice = lax.dynamic_slice_in_dim(down_weight, start, piece_rows, 0)
    ffn_slice = jnp.concatenate([gate_up_slice.reshape(2 * piece_rows, width), down_slice], axis=0)
    ffn_slice = jnp.where(jnp.tile(fresh, 3)[:, None], ffn_slice, 0).astype(BF)

    own_tables = (inward_up, outward_down, expand_up.reshape(adapters, ranks, -1), reduce_down)

    def tables_for(target):
        which = adapter_ids[target]
        return jnp.concatenate(
            [lax.dynamic_index_in_dim(t, which, 0, keepdims=False) for t in own_tables], axis=1
        )

    prepared = [tables_for(sequence)]
    for j in range(1, ways):
        prepared.append(tables_for(core * ways + (place - j) % ways))
    held = barrier((from_next(mixer_slice), mixer_slice, ffn_slice) + tuple(prepared))
    (mixer_1, mixer_slice, ffn_slice), prepared = held[:3], held[3:]
    mixer_2, mixer_3 = from_next(mixer_1), from_last(mixer_slice)
    gathered_near = plane_all(mixer_1)
    tables = [prepared[0]]
    for j in range(1, ways):
        pairs = [(s, (s - j) % ways) for s in range(ways)]
        tables.append(lax.ppermute(prepared[j], "wa", pairs))
    held = barrier((mixer_2, mixer_3, ffn_slice, pad_heads(mixer_out.T)) + tuple(tables[1:]))
    (mixer_2, mixer_3, ffn_slice, out_own), tables[1:] = held[:4], held[4:]
    gathered_rest = plane_all(
        jnp.concatenate(
            [mixer_2[:, :in_width], mixer_3[:, :in_width], mixer_2[:, in_width:], mixer_3[:, in_width:]], axis=1
        )
    )
    cut = [in_width, out_here, hidden_here, hidden_here, hidden_here]
    edges = np.cumsum([0] + cut)
    split_tables = [[t[:, edges[n] : edges[n + 1]] for n in range(5)] for t in tables]
    inward_second = reorder(jnp.concatenate([t[0] for t in split_tables], axis=1))
    outward_first = jnp.concatenate([pad_heads(t[1]) for t in split_tables], axis=1)
    ffn_1, tokens_in, in_own = barrier((from_next(ffn_slice), tokens, reorder(mixer_in)))
    gathered_1 = plane_all(ffn_1)
    in_split = (ways - 2) * in_width
    in_weights = jnp.concatenate([in_own, gathered_near[:, :in_width], gathered_rest[:, :in_split]], axis=1)
    out_weights = jnp.concatenate([out_own, gathered_near[:, in_width:], gathered_rest[:, in_split:]], axis=1)
    x, ffn_slice, in_weights, out_weights, inward_second = barrier(
        (column_exchange(tokens_in), ffn_slice, in_weights, out_weights, inward_second)
    )
    ffn_tables = []
    for j in range(ways):
        chosen = jnp.stack(split_tables[j][2:5])
        if j > 0:
            empty = jnp.zeros((3, ranks, hidden_gap), BF)
            chosen = jnp.concatenate([chosen[..., :gap_at], empty, chosen[..., gap_at:]], axis=2)
        ffn_tables.append(jnp.swapaxes(chosen.reshape(3, ranks, 2, -1), 1, 2))
    ffn_3 = from_last(ffn_slice)

    which = adapter_ids[sequence]

    def pick(table):
        return lax.dynamic_index_in_dim(table, which, 0, keepdims=False)

    inward_first, outward_second = pick(inward_down), pick(outward_up)
    expand_first, reduce_second = pick(expand_down), pick(reduce_up)
    positions = chip * rows + jnp.arange(rows, dtype=jnp.int32)
    keep = (positions < lengths[sequence]).astype(F32)
    keep_row, keep_column = keep[None, :], keep[:, None]

    inputs = x.astype(F32)
    normed = rms(inputs, gain_first).astype(BF)
    enter = dot(normed, inward_first, TURNED).astype(BF)
    packed = (dot(normed, in_weights) + dot(enter, inward_second)).astype(BF)
    taps = pad_heads(jnp.roll(conv_kernel.astype(F32), -place * out_here, axis=1))
    taps = jnp.pad(taps, ((0, 5), (0, 0)))

    def chip_shift(piece, by):
        pairs = [(i, i + by) for i in range(chips) if 0 <= i + by < chips]
        return lax.ppermute(piece, CHIPS, pairs)


    def flip(piece, bit, keep_pair=lambda i: True):
        return lax.ppermute(piece, CHIPS, [(i, i ^ bit) for i in range(chips) if keep_pair(i)])

    def scan_chips(local, sent, want_bit, ahead):
        before = jnp.zeros_like(local)
        total = local
        bit = 1
        while bit < chips:
            if bit > 1:
                sent = total.astype(BF)
            if bit == 2:
                sent = ahead(sent)
            last = 2 * bit >= chips
            got = flip(sent, bit, lambda i: not last or ((i & bit) == 0) == want_bit).astype(F32)
            take = ((chip & bit) != 0) == want_bit
            before = before + jnp.where(take, got, 0.0)
            total = total + got
            bit *= 2
        return before.astype(BF)

    pairs_shape = (PAIRS, PAD)
    ones_column = ones.T
    head_params = pltpu.CompilerParams(dimension_semantics=("arbitrary",))
    packed_spec, head_spec = by_column(rows, PACK), by_column(rows, PAD)
    halo_spec, edge_spec, state_spec = by_column(8, PACK), by_column(8, PAD), by_head(pairs_shape)
    turn_specs = [whole((PAIRS, PAD)), whole((PAIRS, PAD)), whole((PAIRS, 3))]
    pick_specs = [whole((PAD, PAIRS)), whole((PAD, PAIRS))]
    back_specs = [whole((PAIRS, PAD)), whole((PAIRS, PAD)), whole((3, PAIRS))]
    narrow = jax.ShapeDtypeStruct((rows, HEADS * PAD), BF)
    packed_shape = jax.ShapeDtypeStruct((rows, HEADS * PACK), BF)
    state_shape = jax.ShapeDtypeStruct((HEADS,) + pairs_shape, F32)

    state = pl.pallas_call(
        state_kernel,
        grid=(HEADS,),
        in_specs=[packed_spec, whole((1, rows))] + turn_specs,
        out_specs=state_spec,
        out_shape=state_shape,
        compiler_params=head_params,
        name="state",
    )(packed, keep_row, first.T, second.T, ones_column)
    state_sent, last_rows = barrier((state.astype(BF), packed[-8:]))
    ffn_3, cot_in, halo = barrier((ffn_3, cotangent, chip_shift(last_rows, 1)))
    gathered_3 = plane_all(ffn_3)
    cot = column_exchange(cot_in)
    before = scan_chips(state, state_sent, True, lambda sent: sent)
    staged = []
    inside = pl.pallas_call(
        inside_kernel,
        grid=(HEADS,),
        in_specs=[packed_spec, whole((rows, 1))],
        out_specs=head_spec,
        out_shape=jax.ShapeDtypeStruct((rows, HEADS * PAD), F32),
        compiler_params=head_params,
        name="inside",
    )(packed, keep_column)
    held = barrier((ffn_1, cot, inside, before, outward_first) + tuple(ffn_tables))
    (ffn_1, cot, inside, before, outward_first), ffn_tables = held[:5], held[5:]
    ffn_2 = from_next(ffn_1)
    mixed, kept = pl.pallas_call(
        mixer_kernel,
        grid=(HEADS,),
        in_specs=[packed_spec, head_spec, state_spec, halo_spec, edge_spec] + pick_specs + [whole((3, PAIRS))],
        out_specs=[head_spec, head_spec],
        out_shape=[narrow, narrow],
        compiler_params=head_params,
        name="mixer",
    )(packed, inside, before, halo, taps, first, second, ones)

    leave = dot(mixed, outward_first, TURNED).astype(BF)
    residual = inputs + dot(mixed, out_weights, TURNED) + dot(leave, outward_second)
    normed_two = rms(residual, gain_second).astype(BF)
    top = jnp.where(keep_column > 0, cot, jnp.zeros_like(cot))
    top_rank = dot(top, reduce_second, TURNED).astype(BF)
    normed_two, ffn_2, top, top_rank = barrier((normed_two, ffn_2, top, top_rank))
    gathered_far = plane_all(ffn_2)
    expand = dot(normed_two, expand_first, TURNED).astype(BF)

    def own_spec(which):
        return pl.BlockSpec((1, hidden_here // 2, width), lambda n: (which, n, 0))

    def piece_spec(which):
        return pl.BlockSpec((4, 1, piece_rows, width), lambda n: (n, which, 0, 0))

    specs_for = [piece_spec(t) for t in range(3)]

    def parts_of(gathered):
        return (gathered.reshape(8, 3, piece_rows, width),) * 3

    plans = [
        (0, (turned_gate_up, turned_gate_up, down_weight[None]), [own_spec(0), own_spec(1), own_spec(0)]),
        (1, parts_of(gathered_1), specs_for),
        (3, parts_of(gathered_3), specs_for),
        (2, parts_of(gathered_far), specs_for),
    ]
    expand_grads, sums = [None] * ways, ()
    for j, weights, specs in plans:
        *sums, g_gate, g_up, g_reduce = ffn_part(normed_two, top, expand, top_rank, weights, specs, ffn_tables[j], tuple(sums))
        sums, grads = tuple(sums), (g_gate, g_up, g_reduce)
        grads = jnp.swapaxes(jnp.stack(grads), 1, 2).reshape(3, ranks, -1)
        if j > 0:
            grads = jnp.concatenate([grads[..., :gap_at], grads[..., gap_at + hidden_gap :]], axis=2)
        expand_grads[j] = [grads[0], grads[1], grads[2]]
    feed, back, small = sums
    reduce_rank = small[0].astype(BF)
    expand_grad = small[1].astype(BF)
    back = back + dot(expand_grad, expand_first)
    grad_reduce_up = dot(reduce_rank, top, ROWS)
    grad_expand_down = dot(expand_grad, normed_two, ROWS)
    residual_grad = top.astype(F32) + rms_back(residual, gain_second, back)
    branch = residual_grad.astype(BF)
    leave_grad = dot(branch, outward_second, TURNED).astype(BF)
    grad_outward_up = dot(leave, branch, ROWS)
    mixed_grad = (dot(branch, out_weights) + dot(leave_grad, outward_first)).astype(BF)
    grad_outward_down = unpad_heads(dot(leave_grad, mixed, ROWS))

    scaled, back_state, edge = pl.pallas_call(
        back_state_kernel,
        grid=(HEADS,),
        in_specs=[packed_spec, head_spec, head_spec] + turn_specs,
        out_specs=[head_spec, state_spec, edge_spec],
        out_shape=[narrow, state_shape, jax.ShapeDtypeStruct((8, HEADS * PAD), F32)],
        compiler_params=head_params,
        name="back_state",
    )(packed, kept, mixed_grad, first.T, second.T, ones_column)
    hot = (jnp.arange(adapters, dtype=jnp.int32)[:, None] == adapter_ids[None, :]).astype(F32)
    hot = hot.reshape(adapters, 2, ways)
    hot = jnp.where(core == 0, hot, hot[:, ::-1])
    turned = [lax.dynamic_index_in_dim(hot, (place - j) % ways, 2, keepdims=False) for j in range(ways)]
    turned = [lax.dynamic_index_in_dim(jnp.stack(turned, axis=2), (chip % 4) ^ k, 2, keepdims=False) for k in range(4)]
    hot = jnp.stack(turned, axis=2).reshape(adapters, 8)
    same_rank = jnp.eye(ranks, dtype=F32)[None, :, None, :]
    hot_rows = (hot[:, None, :, None] * same_rank).reshape(adapters * ranks, 8 * ranks).astype(BF)

    def exchange_places(pieces):
        got = [pieces(0).astype(BF)]
        for j in range(1, ways):
            pairs = [(s, (s + j) % ways) for s in range(ways)]
            got.append(lax.ppermute(pieces(j).astype(BF), "wa", pairs))
        return jnp.stack(got)

    def exchange_chips(table):
        bit = 4
        while bit < chips:
            table = (table.astype(F32) + flip(table, bit).astype(F32)).astype(BF)
            bit *= 2

        def sequence_at(other):
            return lax.dynamic_index_in_dim(table, (chip % 4) ^ other, 0, keepdims=False)

        summed = sum([flip(sequence_at(k), k).astype(F32) for k in range(1, 4)], sequence_at(0).astype(F32)).astype(BF)
        parts = jnp.concatenate([summed] + [flip(summed, k) for k in range(1, 4)], axis=0)
        parts = jnp.concatenate([parts, lax.ppermute(parts, "c", SWAP)], axis=0)
        return dot(hot_rows, parts).reshape(adapters, ranks, -1)

    shard = width // ways

    def shard_of(table, j):
        return lax.dynamic_slice_in_dim(table, (place + j) % ways * shard, shard, 1)

    any_space = pl.BlockSpec(memory_space=pl.ANY)

    def back_inside(base, scaled, old):
        def shift(spec):
            return pl.BlockSpec(spec.block_shape, lambda h, m=spec.index_map: m(h + base))

        return pl.pallas_call(
            back_inside_kernel if old is None else lambda *refs: back_inside_kernel(*refs[:12], refs[-1]),
            grid=(HEADS // 2,),
            in_specs=[
                shift(packed_spec), shift(head_spec), shift(head_spec), whole((rows, 1)),
                shift(state_spec), shift(halo_spec), shift(edge_spec),
            ]
            + pick_specs
            + back_specs
            + ([] if old is None else [any_space]),
            out_specs=shift(packed_spec),
            out_shape=packed_shape,
            input_output_aliases={} if old is None else {12: 0},
            compiler_params=head_params,
            name="back_inside",
        )(
            packed, scaled, mixed_grad, keep_column, before, halo, taps, first, second, first.T, second.T, ones,
            *(() if old is None else (old,)),
        )

    def inside_first(sent):
        sent, part, again, *rest = barrier((sent, back_inside(0, scaled, None), scaled, feed) + outer_grads)
        staged.append((back_inside(HEADS // 2, again, part), rest))
        return sent

    outer_grads = (grad_outward_down, grad_outward_up, grad_expand_down, grad_reduce_up)
    edge = chip_shift(edge, -1)
    later = scan_chips(back_state, back_state.astype(BF), False, inside_first)
    part, (feed, *outer_grads) = staged[0]
    output = (keep_column * (residual + feed + dot(reduce_rank, reduce_second))).astype(BF)

    def send_back(values):
        return lax.all_to_all(values.reshape(sequences, slot_rows, -1), COLUMN, 0, 0, tiled=True)

    packed_grad = pl.pallas_call(
        back_later_kernel,
        grid=(HEADS,),
        in_specs=[packed_spec, packed_spec, whole((rows, 1)), state_spec, edge_spec, edge_spec]
        + pick_specs
        + back_specs,
        out_specs=packed_spec,
        out_shape=packed_shape,
        compiler_params=head_params,
        name="back_later",
    )(packed, part, keep_column, later, edge, taps, first, second, first.T, second.T, ones)

    packed_grad, back_first = barrier((packed_grad, send_back(output[:, : width // 2])))
    back_last = send_back(after(output[:, width // 2 :], back_first))
    enter_grad = dot(packed_grad, inward_second, TURNED).astype(BF)
    normed_grad = (
        dot(packed_grad, in_weights, TURNED) + dot(enter_grad, inward_first)
    )
    input_grad = (branch.astype(F32) + rms_back(inputs, gain_first, normed_grad)).astype(BF)
    grad_inward_up = dot(dot(enter, packed_grad, ROWS).astype(BF).reshape(-1, PACK), order, TURNED).astype(BF)
    grad_inward_up = grad_inward_up.reshape(ranks, -1)
    grad_inward_down = dot(enter_grad, normed, ROWS)

    places = exchange_places(
        lambda j: jnp.concatenate(
            expand_grads[j]
            + [outer_grads[0][:, j * out_here : (j + 1) * out_here]]
            + [shard_of(t, j) for t in outer_grads[1:]]
            + [grad_inward_up[:, j * in_width : (j + 1) * in_width], shard_of(grad_inward_down, j)],
            axis=1,
        )
    )
    input_grad, places, back_last = barrier((input_grad, places, back_last))
    input_first = send_back(input_grad[:, : width // 2])
    input_last = send_back(after(input_grad[:, width // 2 :], input_first))
    sums = exchange_chips(places)
    at = np.cumsum([0, 2 * hidden_here, hidden_here, out_here, shard, shard, shard, in_width, shard])
    grads = [sums[:, :, at[n] : at[n + 1]] for n in range(8)]
    return (
        jnp.concatenate([back_first, back_last], axis=2).astype(F32),
        jnp.concatenate([input_first, input_last], axis=2).astype(F32),
        grads[7],
        grads[6],
        grads[2],
        grads[3],
        grads[4],
        grads[0].reshape(adapters, ranks, 2, hidden_here),
        grads[1],
        grads[5],
    )


def solution(mesh):
    ways = mesh.shape["wa"]
    split = Mesh(mesh.devices.reshape(-1, 2, 2, 2, ways), EVERY)
    slots = P(None, EVERY, None)
    in_specs = (
        slots, slots, P(), P(), P(), P(), P(),
        P(None, "wa"), P("wa", None), P(None, None, "wa"), P("wa", None),
        P(), P(None, None, "wa"), P(None, None, "wa"), P(), P(), P(None, None, None, "wa"), P(None, None, "wa"), P(),
    )
    third = P(None, None, "wa")
    out_specs = (slots, slots, third, third, third, third, third, P(None, None, None, "wa"), third, third)
    return jax.shard_map(on_device, mesh=split, in_specs=in_specs, out_specs=out_specs, check_vma=False)
```
